32 devices in a mesh: grp: 2 (over y), hgt: 4 (over z), xs: 4 (over x, core).
Axes of the slice: x: 2, y: 2, z: 4, core: 2. Of those that a mesh axis runs over, the one named last changes fastest.
Arguments:
- thermal_field: float32 [512, 16384], P('hgt', ('grp', 'xs')), parts along dimension 1, may hold values from -6 to 6
- thermal_diffusivity: float32 [512, 16384], P('hgt', ('grp', 'xs')), parts along dimension 1, may hold values from 0.2 to 5
- boundary_group_lookup: int32 [128, 6], P('xs'), may hold values from 0 to 40, as said below
- boundary_entry_conductances: float32 [128, 6], P('xs'), may hold values from 0.1 to 1
- exported_boundary_groups: int32 [4, 2, 4], P('xs'), may hold values from 0 to 15, as said below
- domain_group_totals: int32 [4], P('xs'), may hold values from 16 to 32, as said below
- pipe_cavity_indicator: int32 [8192], P('xs'), may hold values 0 or 1
- boundary_vertex_matrix: float32 [64, 64], replicated, may hold values from -0.5 to 0.5
Outputs:
- charged: float32 [512, 16384], P('hgt', ('grp', 'xs')), parts along dimension 1
The draws below stay inside these ranges and needn't reach their ends.
There are 2 independent parts, one for each index of `grp`. The reference program is written for one: setup_inputs(seed, part) draws one part's arguments, and reference() takes and returns one part's arrays. A program takes and returns all parts, laid end to end along the dimension named above; an argument that names none is the same for every part. Nothing has to cross between parts.
Inputs may be any that keep to these rules, and one draw needn't show every extreme that they name: `boundary_group_lookup`: each row lists its own block first, then up to 5 more extended-block indices below 40, then padding entries equal to 40; a row has one to 6 entries that are not padding. `exported_boundary_groups`: the 8 blocks of a partition are distinct and below 16. `domain_group_totals`: some partition has 32 active blocks and some has 16.
All inputs are finite; a program needn't handle non-finite values. No bound on the sum of `pipe_cavity_indicator` on one device may be relied on, other than what follows from the above.
Results may differ from the reference program's by a relative error of at most 0.0001.
Values sent between devices are 32-bit elements; how exact they have to be, the bound alone decides.
No kernel may reach another device: no remote copies, remote signals or barrier semaphores. Data moves between devices by JAX's collectives and lax.ppermute only.
A program may use at most 64 MiB of HBM per device.

```python
import math
import jax
import jax.numpy as jnp
from jax import lax

VERTICAL_SAMPLES = 512
BS = 64
SEND = 4
FMAX = 6
NB = 32
PLANE_VERTICES = 8192
N_HGT = 4
N_XS = 4


def draw_thermal_field(key, part):
    slab = VERTICAL_SAMPLES // N_HGT
    reach = min(20, slab)
    keys = jax.random.split(jax.random.fold_in(key, 41), 7)
    slab_shape = (N_HGT, PLANE_VERTICES)
    top_level = 4.0

    def level(level_key):
        magnitude = jax.random.uniform(level_key, slab_shape, jnp.float32, 1.5, top_level)
        positive = jax.random.bernoulli(jax.random.fold_in(level_key, 1), 0.5, slab_shape)
        return magnitude * jnp.where(positive, 1.0, -1.0).astype(jnp.float32)
    lower_level = level(keys[0])
    middle_level = level(keys[1])
    upper_level = level(keys[2])
    lower_depth = jax.random.randint(keys[3], slab_shape, 1, reach + 1)
    upper_depth = jax.random.randint(keys[4], slab_shape, 1, reach + 1)
    heights = jnp.arange(VERTICAL_SAMPLES)
    slab_of = heights // slab
    from_low = (heights % slab)[:, None]
    from_high = (slab - 1 - heights % slab)[:, None]
    fronts = jnp.where(from_low < lower_depth[slab_of], lower_level[slab_of], jnp.where(from_high < upper_depth[slab_of], upper_level[slab_of], middle_level[slab_of]))
    edge = jnp.minimum(heights % slab, slab - 1 - heights % slab)
    parity = jnp.where(heights % 2 == 0, 1.0, -1.0).astype(jnp.float32)
    near = jnp.where(edge < 6, 1.0, 0.0).astype(jnp.float32)
    rough = jax.random.uniform(keys[5], (VERTICAL_SAMPLES, PLANE_VERTICES), jnp.float32, -1.0, 1.0)
    rough = rough * (parity * near)[:, None]
    bulk = 0.15 * jnp.clip(jax.random.normal(keys[6], (VERTICAL_SAMPLES, PLANE_VERTICES), jnp.float32), -3.0, 3.0)
    return (fronts + rough + bulk).astype(jnp.float32)


def draw_boundary_group_lookup(key, part):
    first_key, second_key = jax.random.split(jax.random.fold_in(key, 11))
    total_rows = N_XS * NB
    entries = jax.random.randint(first_key, (total_rows, FMAX), 0, NB + 2 * SEND)
    local = jnp.arange(total_rows) % NB
    entries = entries.at[:, 0].set(local)
    entries = entries.at[:, 1].set(jnp.where(local < 2 * SEND, NB + local, entries[:, 1]))
    valid = jax.random.randint(second_key, (total_rows,), 1, FMAX + 1)
    valid = jnp.where(local < 2 * SEND, jnp.maximum(valid, 2), valid)
    valid = valid.at[0].set(FMAX)
    valid = valid.at[total_rows - 1].set(1)
    slots = jnp.arange(FMAX)[None, :]
    return jnp.where(slots < valid[:, None], entries, NB + 2 * SEND).astype(jnp.int32)


def draw_exported_boundary_groups(key, part):
    top = NB // 2 - 1
    keys = jax.random.split(jax.random.fold_in(key, 23), N_XS)

    def one_partition(subkey):
        middle = jax.random.permutation(subkey, top - 1) + 1
        chosen = jnp.concatenate([jnp.zeros((1,), jnp.int32), middle[:2 * SEND - 2].astype(jnp.int32), jnp.full((1,), top, jnp.int32)])
        shuffle = jax.random.permutation(jax.random.fold_in(subkey, 5), 2 * SEND)
        return chosen[shuffle]
    return jax.vmap(one_partition)(keys).reshape(N_XS, 2, SEND).astype(jnp.int32)


def draw_domain_group_totals(key, part):
    first_key, second_key = jax.random.split(jax.random.fold_in(key, 31))
    counts = jax.random.randint(first_key, (N_XS,), NB // 2, NB + 1)
    order = jax.random.permutation(second_key, N_XS)
    counts = counts.at[order[0]].set(NB)
    counts = counts.at[order[1]].set(NB // 2)
    return counts.astype(jnp.int32)


def plant(result, rng, least, largest):
    longest = result.shape.index(max(result.shape))
    spots = []
    for shift in (0, 1):
        where = [jax.random.randint(jax.random.fold_in(rng, axis), (), 0, length) for axis, length in enumerate(result.shape)]
        where[longest] = (where[longest] + shift) % result.shape[longest]
        spots.append(tuple(where))
    return result.at[spots[0]].set(least).at[spots[1]].set(largest)


def block_scale(stream_key, dims, pieces, least, high):
    loudness = 1.0
    for position, shards_of in pieces:
        draws = jax.random.uniform(jax.random.fold_in(jax.random.fold_in(stream_key, 6), position), (shards_of,), jnp.float32, least / len(pieces), high / len(pieces))
        loudness = loudness * jnp.repeat(jnp.exp(draws), dims[position] // shards_of).reshape((-1,) + (1,) * (len(dims) - 1 - position))
    return loudness


def bell_draw(key, dims, deviation, most, held_as=jnp.bfloat16):
    values = jax.random.normal(key, dims, jnp.float32) * deviation
    return jnp.minimum(jnp.maximum(values, -most), most).astype(held_as)


def setup_inputs(seed: int = 0, part: int = 0) -> dict:
    splits = jax.random.split(jax.random.key(seed), 9)
    part_keys = jax.random.split(jax.random.fold_in(splits[8], part), 9)
    thermal_field = draw_thermal_field(jax.random.fold_in(jax.random.fold_in(splits[8], part), 71), part)
    thermal_diffusivity = jnp.clip(jnp.exp(math.log(5.0) - 3.218876 * jax.random.uniform(part_keys[1], (VERTICAL_SAMPLES, PLANE_VERTICES), jnp.float32) ** block_scale(part_keys[1], (VERTICAL_SAMPLES, PLANE_VERTICES), ((0, 4), (1, 4)), -0.2, 0.2)), 0.2, 5.0)
    boundary_group_lookup = draw_boundary_group_lookup(jax.random.fold_in(splits[8], 71), part)
    boundary_entry_conductances = jnp.clip(jnp.exp(math.log(1.0) - 2.3025851 * jax.random.uniform(splits[3], (N_XS * NB, FMAX), jnp.float32) ** block_scale(splits[3], (N_XS * NB, FMAX), ((0, 4),), -0.2, 0.2)), 0.1, 1.0)
    exported_boundary_groups = draw_exported_boundary_groups(jax.random.fold_in(splits[8], 71), part)
    domain_group_totals = draw_domain_group_totals(jax.random.fold_in(splits[8], 71), part)
    pipe_cavity_indicator = plant((jax.random.randint(splits[6], (PLANE_VERTICES,), 0, 8) < 1).astype(jnp.int32), jax.random.fold_in(splits[6], 1), 0, 1)
    boundary_vertex_matrix = bell_draw(splits[7], (BS, BS), (2 * BS) ** -0.5, 0.5, jnp.float32)
    return dict(thermal_field=thermal_field, thermal_diffusivity=thermal_diffusivity, boundary_group_lookup=boundary_group_lookup, boundary_entry_conductances=boundary_entry_conductances, exported_boundary_groups=exported_boundary_groups, domain_group_totals=domain_group_totals, pipe_cavity_indicator=pipe_cavity_indicator, boundary_vertex_matrix=boundary_vertex_matrix)


axial_step = 0.5


def cheb_matrix(order):
    index = jnp.arange(order)
    row_f = index[:, None].astype(jnp.float32)
    col_f = index[None, :].astype(jnp.float32)
    angle = math.pi / (2.0 * (order - 1))
    difference = -2.0 * jnp.sin((row_f + col_f) * angle) * jnp.sin((row_f - col_f) * angle)
    ends = (index == 0) | (index == order - 1)
    weight = jnp.where(ends, 2.0, 1.0).astype(jnp.float32)
    parity = jnp.where(((index[:, None] + index[None, :]) % 2) == 0, 1.0, -1.0).astype(jnp.float32)
    off_diag = index[:, None] != index[None, :]
    safe_diff = jnp.where(off_diag, difference, jnp.float32(1.0))
    entries = jnp.where(off_diag, weight[:, None] / weight[None, :] * parity / safe_diff, jnp.float32(0.0))
    entries = entries - jnp.diag(jnp.sum(entries, axis=1))
    mirror = jnp.minimum(index, order - 1 - index).astype(jnp.float32)
    sine = jnp.sin(mirror * (2.0 * angle))
    return (-sine[:, None] * entries / (order - 1)).astype(jnp.float32)


def conduct(present_solution, boundary_group_lookup, boundary_entry_conductances, exported_boundary_groups, boundary_vertex_matrix, mask):
    height = present_solution.shape[0]
    blocked = present_solution.reshape(height, N_XS, NB, BS)
    rows_part = jnp.arange(N_XS)[:, None]
    lower_all = blocked[:, rows_part, exported_boundary_groups[:, 0, :], :]
    upper_all = blocked[:, rows_part, exported_boundary_groups[:, 1, :], :]
    zero_side = jnp.zeros((height, 1, SEND, BS), jnp.float32)
    from_left = jnp.concatenate([zero_side, upper_all[:, :-1]], axis=1)
    from_right = jnp.concatenate([lower_all[:, 1:], zero_side], axis=1)
    empty = jnp.zeros((height, N_XS, 1, BS), jnp.float32)
    extended = jnp.concatenate([blocked, from_left, from_right, empty], axis=2)
    faces_part = boundary_group_lookup.reshape(N_XS, NB, FMAX)
    weights_part = boundary_entry_conductances.reshape(N_XS, NB, FMAX)
    gathered = jnp.zeros((height, N_XS, NB, BS), jnp.float32)
    for slot_index in range(FMAX):
        picked = extended[:, rows_part, faces_part[:, :, slot_index], :]
        gathered = gathered + weights_part[None, :, :, slot_index, None] * picked
    coupled = jnp.dot(gathered.reshape(-1, BS), boundary_vertex_matrix, precision=lax.Precision.HIGHEST,
                      preferred_element_type=jnp.float32).reshape(height, -1)
    return present_solution + mask[None, :] * coupled


def reference(thermal_field, thermal_diffusivity, boundary_group_lookup, boundary_entry_conductances, exported_boundary_groups, domain_group_totals, pipe_cavity_indicator, boundary_vertex_matrix):
    node_ids = jnp.arange(N_XS * NB * BS)
    block_ids = (node_ids // BS) % NB
    part_ids = node_ids // (NB * BS)
    live_groups = block_ids < domain_group_totals[part_ids]
    mask = jnp.where(live_groups & (pipe_cavity_indicator == 0), 1.0, 0.0).astype(jnp.float32)
    operator = cheb_matrix(VERTICAL_SAMPLES)
    present_solution = jnp.where(live_groups[None, :], thermal_field, jnp.float32(0.0))
    for repeat in range(2):
        moved = conduct(present_solution, boundary_group_lookup, boundary_entry_conductances, exported_boundary_groups, boundary_vertex_matrix, mask)
        slope = jnp.dot(operator, moved, precision=lax.Precision.HIGHEST, preferred_element_type=jnp.float32)
        second = jnp.dot(operator, thermal_diffusivity * slope, precision=lax.Precision.HIGHEST,
                         preferred_element_type=jnp.float32)
        present_solution = moved + axial_step * mask[None, :] * second
    return present_solution
```

```python
import functools
import math

import numpy as np
import jax
import jax.numpy as jnp
from jax import lax
from jax.experimental import pallas as pl
from jax.experimental.pallas import tpu as pltpu
from jax.sharding import PartitionSpec as P

axial_step = 0.5
lanes = 128
near_rows = 16
far_rows = 8
carried_rows = 24
unit_roundoff = 2.0**-24


def cheb_exact(order):
    index = np.arange(order, dtype=np.float64)
    angle = math.pi / (2.0 * (order - 1))
    row, col = index[:, None], index[None, :]
    difference = -2.0 * np.sin((row + col) * angle) * np.sin((row - col) * angle)
    weight = np.ones(order)
    weight[0] = weight[-1] = 2.0
    parity = np.where((row + col) % 2 == 0, 1.0, -1.0)
    off_diag = row != col
    entries = np.where(
        off_diag, weight[:, None] / weight[None, :] * parity / np.where(off_diag, difference, 1.0), 0.0
    )
    entries = entries - np.diag(entries.sum(axis=1))
    sine = np.sin(np.minimum(index, order - 1 - index) * (2.0 * angle))
    return -sine[:, None] * entries / (order - 1)


def row_basis(block, rank):
    return np.linalg.svd(block, full_matrices=False)[2][:rank]


@functools.lru_cache(maxsize=None)
def slab_factors(order, spans):
    slab = order // spans
    if spans & (spans - 1) or spans > 4 or slab < 4 * near_rows:
        return None
    full = cheb_exact(order)
    block = lambda s, t: full[s * slab : (s + 1) * slab, t * slab : (t + 1) * slab]
    ranks = [near_rows if any(abs(s - (s ^ x)) == 1 for s in range(spans)) else far_rows for x in range(1, spans)]
    first, joint = {}, {}
    carried, onward, left = {}, {}, {}
    for s in range(spans):
        others = [t for t in range(spans) if t != s]
        u, sigma, vt = np.linalg.svd(np.concatenate([block(s, t) for t in others], axis=1), full_matrices=False)
        left[s] = u[:, :carried_rows]
        rows = sigma[:carried_rows, None] * vt[:carried_rows]
        carried[s] = {t: rows[:, i * slab : (i + 1) * slab] for i, t in enumerate(others)}
        onward[s] = sum(carried[s][t] @ full[t * slab : (t + 1) * slab] for t in others)
        for t in others:
            first[s, t] = row_basis(block(s, t), ranks[(s ^ t) - 1])
            joint[s, t] = row_basis(
                np.concatenate([block(s, t), onward[s][:, t * slab : (t + 1) * slab]], axis=0), ranks[(s ^ t) - 1]
            )
    send_first, send_joint, apply_first, apply_joint, apply_carried = [], [], [], [], []
    for s in range(spans):
        partners = [s ^ x for x in range(1, spans)]
        send_first.append(np.concatenate([first[t, s] for t in partners], axis=0))
        send_joint.append(np.concatenate([joint[t, s] for t in partners], axis=0))
        own = onward[s][:, s * slab : (s + 1) * slab]
        apply_first.append(
            np.block(
                [
                    [block(s, s)] + [block(s, t) @ first[s, t].T for t in partners],
                    [np.zeros_like(own)] + [carried[s][t] @ first[s, t].T for t in partners],
                ]
            )
        )
        apply_joint.append(
            np.block(
                [
                    [block(s, s)] + [block(s, t) @ joint[s, t].T for t in partners],
                    [own] + [onward[s][:, t * slab : (t + 1) * slab] @ joint[s, t].T for t in partners],
                ]
            )
        )
        apply_carried.append(np.concatenate([block(s, s), left[s]], axis=1))
    stack = lambda parts: np.stack(parts).astype(np.float32)
    return dict(
        ranks=ranks,
        send_first=stack(send_first),
        send_joint=stack(send_joint),
        apply_first=stack(apply_first),
        apply_joint=stack(apply_joint),
        apply_carried=stack(apply_carried),
    )


def product(left, right):
    return jnp.dot(left, right, precision=lax.Precision.HIGHEST, preferred_element_type=jnp.float32)


def low_half():
    return lax.broadcasted_iota(jnp.int32, (1, lanes), 1) < lanes // 2


def take_faces(source, exported, out, side):
    half = lanes // 2
    for tile in range(out.shape[1] // lanes):
        parts = []
        for place in range(2):
            index = exported[side, 2 * tile + place]
            value = source[:, pl.ds(pl.multiple_of(index // 2 * lanes, lanes), lanes)]
            parts.append(jnp.where(index % 2 == place, value, pltpu.roll(value, half, 1)))
        out[:, tile * lanes : (tile + 1) * lanes] = jnp.where(low_half(), parts[0], parts[1])


def faces_kernel(exported, total, field, pipe, matrix, lower, upper, mask, spread):
    take_faces(field, exported, lower, 0)
    take_faces(field, exported, upper, 1)
    width = matrix.shape[0]
    block = lax.broadcasted_iota(jnp.int32, mask.shape, 1) // width
    mask[...] = jnp.where((block < total[0]) & (pipe[...] == 0), 1.0, 0.0).astype(jnp.float32)
    copies = spread.shape[0] // width
    wide = jnp.concatenate([matrix[...]] * copies, axis=1)
    tall = jnp.concatenate([wide] * copies, axis=0)
    row = lax.broadcasted_iota(jnp.int32, spread.shape, 0) // width
    col = lax.broadcasted_iota(jnp.int32, spread.shape, 1) // width
    spread[...] = jnp.where(row == col, tall, 0.0)


def fill_extended(extended, tile, value):
    extended[0, tile] = value
    extended[1, tile] = pltpu.roll(value, lanes // 2, 1)


def spread_faces(lookup, conductance, own, left, right, mask, spread, extended, gathered, out):
    tiles = out.shape[1] // lanes
    rim = left.shape[1] // lanes
    half = low_half()
    for tile in range(tiles):
        fill_extended(extended, tile, own(tile))
    for tile in range(rim):
        piece = slice(tile * lanes, (tile + 1) * lanes)
        fill_extended(extended, tiles + tile, left[:, piece])
        fill_extended(extended, tiles + rim + tile, right[:, piece])
    fill_extended(extended, tiles + 2 * rim, jnp.zeros(extended.shape[2:], jnp.float32))
    wide = spread.shape[0]
    for tile in range(tiles):
        low, high = 2 * tile, 2 * tile + 1
        total = jnp.where(half, conductance[0, low], conductance[0, high]) * extended[0, tile]
        for slot in range(1, lookup.shape[0]):
            first, second = lookup[slot, low], lookup[slot, high]
            value = jnp.where(half, extended[first % 2, first // 2], extended[1 - second % 2, second // 2])
            total = total + jnp.where(half, conductance[slot, low], conductance[slot, high]) * value
        gathered[:, tile * lanes : (tile + 1) * lanes] = total
    for start in range(0, out.shape[1], wide):
        piece = slice(start, start + wide)
        own_piece = jnp.concatenate([extended[0, start // lanes + i] for i in range(wide // lanes)], axis=1)
        out[:, piece] = own_piece + mask[:, piece] * product(gathered[:, piece], spread[...])


def chunks(width):
    step = min(width, 512)
    return [slice(start, start + step) for start in range(0, width, step)]


def send_rows(rows, source, outs, piece):
    moved = product(rows, source)
    start = 0
    for out in outs:
        out[:, piece] = moved[start : start + out.shape[0]]
        start += out.shape[0]


def first_kernel(spans, where, lookup, conductance, total, field, left, right, mask, spread, send, *refs):
    out, outs, (extended, gathered) = refs[0], refs[1:spans], refs[spans:]
    width = lanes // 2

    def own(tile):
        block = 2 * tile + lax.broadcasted_iota(jnp.int32, (1, lanes), 1) // width
        return jnp.where(block < total[0], field[:, tile * lanes : (tile + 1) * lanes], 0.0)

    spread_faces(lookup, conductance, own, left, right, mask, spread, extended, gathered, out)
    rows = send[where[0]]
    for piece in chunks(out.shape[1]):
        send_rows(rows, out[:, piece], outs, piece)


def flux_kernel(spans, where, field, *refs):
    got, (kappa, apply, send), outs = refs[: spans - 1], refs[spans - 1 : spans + 2], refs[spans + 2 :]
    flux, carried, outs = outs[0], outs[1], outs[2:]
    slab = field.shape[0]
    rows = send[where[0]]
    weights = apply[where[0]]
    for piece in chunks(field.shape[1]):
        values = jnp.concatenate([field[:, piece]] + [ref[:, piece] for ref in got], axis=0)
        slope = product(weights, values)
        carried[:, piece] = slope[slab:]
        value = kappa[:, piece] * slope[:slab]
        flux[:, piece] = value
        send_rows(rows, value, outs, piece)


def close_kernel(spans, where, exported, field, carried, flux, *refs):
    got, (mask, apply), (out, lower, upper) = refs[: spans - 1], refs[spans - 1 : spans + 1], refs[spans + 1 :]
    slab = field.shape[0]
    weights = apply[where[0]]
    for piece in chunks(field.shape[1]):
        values = jnp.concatenate([flux[:, piece]] + [ref[:, piece] for ref in got], axis=0)
        step = axial_step * mask[:, piece] * product(weights, values)
        out[:slab, piece] = field[:, piece] + step[:slab]
        out[slab:, piece] = carried[:, piece] + step[slab:]
    take_faces(out, exported, lower, 0)
    take_faces(out, exported, upper, 1)


def second_kernel(spans, where, lookup, conductance, field, left, right, mask, spread, kappa, apply, send, *refs):
    out, flux, outs, (moved, extended, gathered) = refs[0], refs[1], refs[2 : spans + 1], refs[spans + 1 :]
    own = lambda tile: field[:, tile * lanes : (tile + 1) * lanes]
    spread_faces(lookup, conductance, own, left, right, mask, spread, extended, gathered, moved)
    slab = out.shape[0]
    rows = send[where[0]]
    weights = apply[where[0]]
    for piece in chunks(out.shape[1]):
        values = moved[:, piece]
        out[:, piece] = values[:slab]
        value = kappa[:, piece] * product(weights, values)
        flux[:, piece] = value
        send_rows(rows, value, outs, piece)


def last_kernel(spans, where, field, flux, *refs):
    got, (mask, apply, out) = refs[: spans - 1], refs[spans - 1 :]
    weights = apply[where[0], : field.shape[0]]
    for piece in chunks(field.shape[1]):
        values = jnp.concatenate([flux[:, piece]] + [ref[:, piece] for ref in got], axis=0)
        out[:, piece] = field[:, piece] + axial_step * mask[:, piece] * product(weights, values)


def call(kernel, scalars, arrays, shapes, scratch=(), flops=0):
    scalar = pl.BlockSpec(memory_space=pltpu.SMEM)
    vector = pl.BlockSpec(memory_space=pltpu.VMEM)
    size = sum(4 * math.prod(shape) for shape in shapes) + sum(4 * a.size for a in arrays)
    return pl.pallas_call(
        kernel,
        in_specs=[scalar] * len(scalars) + [vector] * len(arrays),
        out_specs=[vector] * len(shapes),
        out_shape=[jax.ShapeDtypeStruct(shape, jnp.float32) for shape in shapes],
        scratch_shapes=[pltpu.VMEM(shape, jnp.float32) for shape in scratch],
        compiler_params=pltpu.CompilerParams(vmem_limit_bytes=32 * 2**20),
        cost_estimate=pl.CostEstimate(flops=flops, bytes_accessed=size, transcendentals=0),
    )(*scalars, *arrays)


def trade_faces(lower, upper):
    count = lax.axis_size("xs")
    ends = count - 1
    from_left = lax.ppermute(upper, "xs", [(i, i + 1) for i in range(ends)])
    from_right = lax.ppermute(lower, "xs", [(i + 1, i) for i in range(ends)])
    return from_left, from_right


def trade_slabs(parts):
    count = lax.axis_size("hgt")
    return [lax.ppermute(part, "hgt", [(i, i ^ x) for i in range(count)]) for x, part in enumerate(parts, 1)]


def slab_body(factors, field, kappa, lookup, conductance, exported, totals, pipe, matrix):
    slab, nodes = field.shape
    spans = lax.axis_size("hgt")
    ranks = factors["ranks"]
    rim = exported.shape[2] * matrix.shape[0]
    where = jnp.full((1,), lax.axis_index("hgt"), jnp.int32)
    lookup, conductance = lookup.T, conductance.T
    exported = exported.reshape(exported.shape[1:])
    tall = slab + carried_rows
    tiles = (nodes + 2 * rim) // lanes + 1
    moved = [(rank, nodes) for rank in ranks]
    flops = 2 * slab * (slab + sum(ranks)) * nodes
    lower, upper, mask, spread = call(
        faces_kernel,
        [exported, totals],
        [field, pipe.reshape(1, nodes), matrix],
        [(slab, rim), (slab, rim), (1, nodes), (2 * lanes, 2 * lanes)],
    )
    left, right = trade_faces(lower, upper)
    state, *rows = call(
        functools.partial(first_kernel, spans),
        [where, lookup, conductance, totals],
        [field, left, right, mask, spread, factors["send_first"]],
        [(slab, nodes)] + moved,
        [(2, tiles, slab, lanes), (slab, nodes)],
        flops,
    )
    rows = trade_slabs(rows)
    flux, carried, *rows = call(
        functools.partial(flux_kernel, spans),
        [where],
        [state, *rows, kappa, factors["apply_first"], factors["send_joint"]],
        [(slab, nodes), (carried_rows, nodes)] + moved,
        flops=flops,
    )
    rows = trade_slabs(rows)
    state, lower, upper = call(
        functools.partial(close_kernel, spans),
        [where, exported],
        [state, carried, flux, *rows, mask, factors["apply_joint"]],
        [(tall, nodes), (tall, rim), (tall, rim)],
        flops=flops,
    )
    left, right = trade_faces(lower, upper)
    state, flux, *rows = call(
        functools.partial(second_kernel, spans),
        [where, lookup, conductance],
        [state, left, right, mask, spread, kappa, factors["apply_carried"], factors["send_first"]],
        [(slab, nodes), (slab, nodes)] + moved,
        [(tall, nodes), (2, tiles, tall, lanes), (tall, nodes)],
        flops,
    )
    rows = trade_slabs(rows)
    (state,) = call(
        functools.partial(last_kernel, spans),
        [where],
        [state, flux, *rows, mask, factors["apply_first"]],
        [(slab, nodes)],
        flops=flops,
    )
    return state


def padded_2(cells, sides, width):
    for axis, dim in sides:
        count = lax.axis_size(axis)
        ends = count - 1
        head = lax.slice_in_dim(cells, 0, width, axis=dim)
        tail = lax.slice_in_dim(cells, cells.shape[dim] - width, cells.shape[dim], axis=dim)
        cells = jnp.concatenate(
            [
                lax.ppermute(tail, axis, [(i, (i + 1) % count) for i in range(ends)]),
                cells,
                lax.ppermute(head, axis, [((i + 1) % count, i) for i in range(ends)]),
            ],
            axis=dim,
        )
    return cells


def cheb_matrix(order):
    index = jnp.arange(order)
    row_f = index[:, None].astype(jnp.float32)
    col_f = index[None, :].astype(jnp.float32)
    angle = math.pi / (2.0 * (order - 1))
    difference = -2.0 * jnp.sin((row_f + col_f) * angle) * jnp.sin((row_f - col_f) * angle)
    ends = (index == 0) | (index == order - 1)
    weight = jnp.where(ends, 2.0, 1.0).astype(jnp.float32)
    parity = jnp.where((index[:, None] + index[None, :]) % 2 == 0, 1.0, -1.0).astype(jnp.float32)
    off_diag = index[:, None] != index[None, :]
    safe_diff = jnp.where(off_diag, difference, jnp.float32(1.0))
    entries = jnp.where(
        off_diag, weight[:, None] / weight[None, :] * parity / safe_diff, jnp.float32(0.0)
    )
    entries = entries - jnp.diag(jnp.sum(entries, axis=1))
    mirror = jnp.minimum(index, order - 1 - index).astype(jnp.float32)
    sine = jnp.sin(mirror * (2.0 * angle))
    return -sine[:, None] * entries / (order - 1)


def slot_sum(source, indices, boundary_entry_conductances, total):
    for slot_index in range(indices.shape[1]):
        picked = source[:, indices[:, slot_index], :]
        total = total + boundary_entry_conductances[None, :, slot_index, None] * picked
    return total


def conduct(
    present_solution,
    boundary_group_lookup,
    boundary_entry_conductances,
    exported_boundary_groups,
    spread,
    slab_mask,
    width,
):
    height, plane_vertices = present_solution.shape
    blocks = plane_vertices // width
    face_count = exported_boundary_groups.shape[2]
    blocked = present_solution.reshape(height, blocks, width)
    outgoing = jnp.concatenate(
        [
            blocked[:, exported_boundary_groups[0, 0], :],
            blocked[:, exported_boundary_groups[0, 1], :],
        ],
        axis=1,
    )
    outgoing = outgoing.reshape(height, 2 * face_count * width)
    rim_width = face_count * width
    padded = padded_2(outgoing, (("xs", 1),), rim_width)
    from_left = padded[:, :rim_width].reshape(height, face_count, width)
    from_right = padded[:, padded.shape[1] - rim_width :].reshape(height, face_count, width)
    empty = jnp.zeros((height, 1, width), jnp.float32)
    gathered = jnp.zeros((height, blocks, width), jnp.float32)
    extended = jnp.concatenate([blocked, from_left, from_right, empty], axis=1)
    gathered = slot_sum(extended, boundary_group_lookup, boundary_entry_conductances, gathered)
    coupled = jnp.dot(
        gathered.reshape(-1, spread.shape[0]),
        spread,
        precision=lax.Precision.HIGHEST,
        preferred_element_type=jnp.float32,
    ).reshape(height, plane_vertices)
    return present_solution + slab_mask[None, :] * coupled


def axial(column_field, column_kappa, operator, column_mask):
    slope = jnp.dot(
        operator, column_field, precision=lax.Precision.HIGHEST, preferred_element_type=jnp.float32
    )
    second = jnp.dot(
        operator,
        column_kappa * slope,
        precision=lax.Precision.HIGHEST,
        preferred_element_type=jnp.float32,
    )
    return column_field + axial_step * column_mask[None, :] * second


def to_columns(moved):
    return lax.all_to_all(moved, "hgt", split_axis=1, concat_axis=0, tiled=True)


def to_slabs(result):
    return lax.all_to_all(result, "hgt", split_axis=0, concat_axis=1, tiled=True)


def column_body(
    thermal_field,
    thermal_diffusivity,
    boundary_group_lookup,
    boundary_entry_conductances,
    exported_boundary_groups,
    domain_group_totals,
    pipe_cavity_indicator,
    boundary_vertex_matrix,
):
    layer_sample_number, plane_vertices = thermal_field.shape
    width = boundary_vertex_matrix.shape[0]
    group_size = max(1, 128 // width)
    spread = jnp.kron(jnp.eye(group_size, dtype=jnp.float32), boundary_vertex_matrix)
    block_ids = jnp.arange(plane_vertices) // width
    live_groups = block_ids < domain_group_totals[0]
    slab_mask = jnp.where(live_groups & (pipe_cavity_indicator == 0), 1.0, 0.0).astype(jnp.float32)
    spans = lax.axis_size("hgt")
    column_count = plane_vertices // spans
    column_start = lax.axis_index("hgt") * column_count
    column_mask = lax.dynamic_slice_in_dim(slab_mask, column_start, column_count, 0)
    operator = cheb_matrix(layer_sample_number * spans)
    present_solution = jnp.where(live_groups[None, :], thermal_field, jnp.float32(0.0))
    moved = conduct(
        present_solution,
        boundary_group_lookup,
        boundary_entry_conductances,
        exported_boundary_groups,
        spread,
        slab_mask,
        width,
    )
    column_field, kappa_fixed = (
        lax.all_to_all(moved, "hgt", split_axis=1, concat_axis=0, tiled=True),
        lax.all_to_all(thermal_diffusivity, "hgt", split_axis=1, concat_axis=0, tiled=True),
    )
    result = axial(column_field, kappa_fixed, operator, column_mask)
    present_solution = to_slabs(result)
    moved = conduct(
        present_solution,
        boundary_group_lookup,
        boundary_entry_conductances,
        exported_boundary_groups,
        spread,
        slab_mask,
        width,
    )
    result = axial(to_columns(moved), kappa_fixed, operator, column_mask)
    present_solution = to_slabs(result)
    return present_solution


def body(field, kappa, lookup, conductance, exported, totals, pipe, matrix):
    spans = lax.axis_size("hgt")
    factors = slab_factors(field.shape[0] * spans, spans)
    args = (field, kappa, lookup, conductance, exported, totals, pipe, matrix)
    if factors is None or 2 * matrix.shape[0] != lanes:
        return column_body(*args)
    return slab_body(factors, *args)


def solution(mesh):
    in_specs = (
        P("hgt", ("grp", "xs")),
        P("hgt", ("grp", "xs")),
        P("xs", None),
        P("xs", None),
        P("xs", None, None),
        P("xs"),
        P("xs"),
        P(),
    )
    out_specs = P("hgt", ("grp", "xs"))
    return jax.shard_map(body, mesh=mesh, in_specs=in_specs, out_specs=out_specs, check_vma=False)
```

```python
import functools
import math

import numpy as np
import jax
import jax.numpy as jnp
from jax import lax
from jax.experimental import pallas as pl
from jax.experimental.pallas import tpu as pltpu
from jax.sharding import PartitionSpec as P

axial_step = 0.5
lanes = 128
near_rows = 16
far_rows = 8
carried_rows = 24
unit_roundoff = 2.0**-24


def cheb_exact(order):
    index = np.arange(order, dtype=np.float64)
    angle = math.pi / (2.0 * (order - 1))
    row, col = index[:, None], index[None, :]
    difference = -2.0 * np.sin((row + col) * angle) * np.sin((row - col) * angle)
    weight = np.ones(order)
    weight[0] = weight[-1] = 2.0
    parity = np.where((row + col) % 2 == 0, 1.0, -1.0)
    off_diag = row != col
    entries = np.where(
        off_diag, weight[:, None] / weight[None, :] * parity / np.where(off_diag, difference, 1.0), 0.0
    )
    entries = entries - np.diag(entries.sum(axis=1))
    sine = np.sin(np.minimum(index, order - 1 - index) * (2.0 * angle))
    return -sine[:, None] * entries / (order - 1)


def row_basis(block, rank):
    return np.linalg.svd(block, full_matrices=False)[2][:rank]


@functools.lru_cache(maxsize=None)
def slab_factors(order, spans):
    slab = order // spans
    if spans & (spans - 1) or spans > 4 or slab < 4 * near_rows:
        return None
    full = cheb_exact(order)
    block = lambda s, t: full[s * slab : (s + 1) * slab, t * slab : (t + 1) * slab]
    ranks = [near_rows if any(abs(s - (s ^ x)) == 1 for s in range(spans)) else far_rows for x in range(1, spans)]
    first, joint = {}, {}
    carried, onward, left = {}, {}, {}
    for s in range(spans):
        others = [t for t in range(spans) if t != s]
        u, sigma, vt = np.linalg.svd(np.concatenate([block(s, t) for t in others], axis=1), full_matrices=False)
        left[s] = u[:, :carried_rows]
        rows = sigma[:carried_rows, None] * vt[:carried_rows]
        carried[s] = {t: rows[:, i * slab : (i + 1) * slab] for i, t in enumerate(others)}
        onward[s] = sum(carried[s][t] @ full[t * slab : (t + 1) * slab] for t in others)
        for t in others:
            first[s, t] = row_basis(block(s, t), ranks[(s ^ t) - 1])
            joint[s, t] = row_basis(
                np.concatenate([block(s, t), onward[s][:, t * slab : (t + 1) * slab]], axis=0), ranks[(s ^ t) - 1]
            )
    send_first, send_joint, apply_first, apply_joint, apply_carried = [], [], [], [], []
    for s in range(spans):
        partners = [s ^ x for x in range(1, spans)]
        send_first.append(np.concatenate([first[t, s] for t in partners], axis=0))
        send_joint.append(np.concatenate([joint[t, s] for t in partners], axis=0))
        own = onward[s][:, s * slab : (s + 1) * slab]
        apply_first.append(
            np.block(
                [
                    [block(s, s)] + [block(s, t) @ first[s, t].T for t in partners],
                    [np.zeros_like(own)] + [carried[s][t] @ first[s, t].T for t in partners],
                ]
            )
        )
        apply_joint.append(
            np.block(
                [
                    [block(s, s)] + [block(s, t) @ joint[s, t].T for t in partners],
                    [own] + [onward[s][:, t * slab : (t + 1) * slab] @ joint[s, t].T for t in partners],
                ]
            )
        )
        apply_carried.append(np.concatenate([block(s, s), left[s]], axis=1))
    stack = lambda parts: np.stack(parts).astype(np.float32)
    return dict(
        ranks=ranks,
        send_first=stack(send_first),
        send_joint=stack(send_joint),
        apply_first=stack(apply_first),
        apply_joint=stack(apply_joint),
        apply_carried=stack(apply_carried),
    )


def product(left, right):
    return jnp.dot(left, right, precision=lax.Precision.HIGHEST, preferred_element_type=jnp.float32)


def low_half():
    return lax.broadcasted_iota(jnp.int32, (1, lanes), 1) < lanes // 2


def tile_at(tile):
    return slice(tile * lanes, (tile + 1) * lanes)


def chunks(width):
    step = min(width, 512)
    return [slice(start, start + step) for start in range(0, width, step)]


def load(copies, sems):
    started = [pltpu.make_async_copy(source, target, sems.at[i]) for i, (source, target) in enumerate(copies)]
    for copy in started:
        copy.start()
    return started


def sides():
    first = 1 - lax.axis_index("xs") % 2
    return first, 1 - first


def take_face(source, exported, side):
    tiles = []
    for tile in range(exported.shape[1] // 2):
        parts = []
        for place in range(2):
            index = exported[side, 2 * tile + place]
            value = source[:, pl.ds(pl.multiple_of(index // 2 * lanes, lanes), lanes)]
            parts.append(jnp.where(index % 2 == place, value, pltpu.roll(value, lanes // 2, 1)))
        tiles.append(jnp.where(low_half(), parts[0], parts[1]))
    return jnp.concatenate(tiles, axis=1)


def faces_kernel(exported, field, first, second, faces, near, sems):
    got = load([(exported, faces), (field.at[:, pl.ds(0, near.shape[1])], near)], sems)
    for copy in got:
        copy.wait()
    for side, out in zip(sides(), (first, second)):
        out[...] = take_face(near, faces, side)


def prepare_kernel(sizes, total, pipe, matrix, field, *refs):
    count = len(sizes)
    stacks, (mask, spread, state, moments), outs = refs[:count], refs[count : count + 4], refs[count + 4 : 2 * count + 4]
    (sems,) = refs[2 * count + 4 :]
    where = lax.axis_index("hgt")
    got = load([(stack.at[where], out) for stack, out in zip(stacks, outs)], sems)
    width = matrix.shape[0]
    copies = spread.shape[0] // width
    wide = jnp.concatenate([matrix[...]] * copies, axis=1)
    tall = jnp.concatenate([wide] * copies, axis=0)
    row = lax.broadcasted_iota(jnp.int32, spread.shape, 0) // width
    col = lax.broadcasted_iota(jnp.int32, spread.shape, 1) // width
    spread[...] = jnp.where(row == col, tall, 0.0)
    for copy in got:
        copy.wait()
    block = lax.broadcasted_iota(jnp.int32, mask.shape, 1) // width
    live = block < total[0]
    mask[...] = jnp.where(live & (pipe[...] == 0), 1.0, 0.0).astype(jnp.float32)
    for piece in chunks(field.shape[1]):
        state[:, piece] = jnp.where(live[:, piece], field[:, piece], 0.0)
        moments[:, piece] = product(outs[0][...], state[:, piece])


def fill(extended, tile, value):
    extended[0, tile] = value
    extended[1, tile] = pltpu.roll(value, lanes // 2, 1)


def fill_own(extended, own):
    tiles = own.shape[1] // lanes
    for tile in range(tiles):
        fill(extended, tile, own[:, tile_at(tile)])
    fill(extended, extended.shape[1] - 1, jnp.zeros(extended.shape[2:], jnp.float32))


def fill_rim(extended, first, second):
    rim = first.shape[1] // lanes
    start = extended.shape[1] - 1 - 2 * rim
    for side, values in zip(sides(), (first, second)):
        for tile in range(rim):
            fill(extended, start + side * rim + tile, values[:, tile_at(tile)])


def conducted(lookup, conductance, mask, spread, extended, gathered, pieces):
    half = low_half()
    per = spread.shape[0] // lanes
    for piece in pieces:
        start = piece.start // lanes
        for tile in range(start, piece.stop // lanes):
            low, high = 2 * tile, 2 * tile + 1
            total = jnp.where(half, conductance[0, low], conductance[0, high]) * extended[0, tile]
            for slot in range(1, lookup.shape[0]):
                one, two = lookup[slot, low], lookup[slot, high]
                value = jnp.where(half, extended[one % 2, one // 2], extended[1 - two % 2, two // 2])
                total = total + jnp.where(half, conductance[slot, low], conductance[slot, high]) * value
            gathered[:, tile_at(tile)] = total
        moved = []
        for tile in range(start, piece.stop // lanes, per):
            part = slice(tile * lanes, (tile + per) * lanes)
            own = jnp.concatenate([extended[0, tile + i] for i in range(per)], axis=1)
            moved.append(own + mask[:, part] * product(gathered[:, part], spread[...]))
        yield piece, jnp.concatenate(moved, axis=1)


def store_rows(moved, outs, piece):
    start = 0
    for out in outs:
        out[:, piece] = moved[start : start + out.shape[0]]
        start += out.shape[0]


def stacked(refs, piece):
    return jnp.concatenate([ref[:, piece] for ref in refs], axis=0)


def moments_kernel(lookup, conductance, moments, first, second, mask, spread, send, *refs):
    outs, (table, weight, extended, gathered, sems) = refs[:-5], refs[-5:]
    got = load([(lookup, table), (conductance, weight)], sems)
    fill_own(extended, moments)
    fill_rim(extended, product(send[...], first[...]), product(send[...], second[...]))
    for copy in got:
        copy.wait()
    for piece, values in conducted(table, weight, mask, spread, extended, gathered, chunks(moments.shape[1])):
        store_rows(values, outs, piece)


def first_kernel(lookup, conductance, field, first, second, mask, spread, apply, out, slope, *scratch):
    table, weight, extended, gathered, sems = scratch
    got = load([(lookup, table), (conductance, weight)], sems)
    fill_own(extended, field)
    fill_rim(extended, first, second)
    for copy in got:
        copy.wait()
    local = apply[: field.shape[0], : field.shape[0]]
    for piece, values in conducted(table, weight, mask, spread, extended, gathered, chunks(field.shape[1])):
        out[:, piece] = values
        slope[:, piece] = product(local, values)


def flux_kernel(spans, slope, *refs):
    got, (kappa, apply, send), (flux, carried), outs = (
        refs[: spans - 1],
        refs[spans - 1 : spans + 2],
        refs[spans + 2 : spans + 4],
        refs[spans + 4 :],
    )
    slab = slope.shape[0]
    weights = apply[:, slab:]
    for piece in chunks(slope.shape[1]):
        far = product(weights, stacked(got, piece))
        carried[:, piece] = far[slab:]
        value = kappa[:, piece] * (slope[:, piece] + far[:slab])
        flux[:, piece] = value
        store_rows(product(send[...], value), outs, piece)


def local_kernel(field, carried, flux, mask, apply, out):
    slab = field.shape[0]
    weights = apply[:, :slab]
    for piece in chunks(field.shape[1]):
        step = axial_step * mask[:, piece] * product(weights, flux[:, piece])
        out[:slab, piece] = field[:, piece] + step[:slab]
        out[slab:, piece] = carried[:, piece] + step[slab:]


def rim_kernel(spans, exported, base, mask, apply, *refs):
    got, (first, second, faces, sems) = refs[: spans - 1], refs[spans - 1 :]
    (copy,) = load([(exported, faces)], sems)
    copy.wait()
    weights = apply[:, apply.shape[1] - sum(ref.shape[0] for ref in got) :]
    for side, out in zip(sides(), (first, second)):
        rows = jnp.concatenate([take_face(ref, faces, side) for ref in got], axis=0)
        out[...] = take_face(base, faces, side) + axial_step * take_face(mask, faces, side) * product(weights, rows)


def close_kernel(spans, base, mask, apply, onward, *refs):
    got, (out, slope) = refs[: spans - 1], refs[spans - 1 :]
    slab = out.shape[0]
    weights = apply[:, slab:]
    for piece in chunks(base.shape[1]):
        values = base[:, piece] + axial_step * mask[:, piece] * product(weights, stacked(got, piece))
        out[:, piece] = values[:slab]
        slope[:, piece] = product(onward[...], values)


def second_kernel(lookup, conductance, slope, first, second, mask, spread, kappa, onward, send, flux, *refs):
    outs, (table, weight, extended, gathered, sems) = refs[:-5], refs[-5:]
    got = load([(lookup, table), (conductance, weight)], sems)
    fill_own(extended, slope)
    fill_rim(extended, product(onward[...], first[...]), product(onward[...], second[...]))
    for copy in got:
        copy.wait()
    for piece, values in conducted(table, weight, mask, spread, extended, gathered, chunks(slope.shape[1])):
        value = kappa[:, piece] * values
        flux[:, piece] = value
        store_rows(product(send[...], value), outs, piece)


def rest_kernel(lookup, conductance, field, flux, first, second, mask, spread, apply, out, *scratch):
    table, weight, extended, gathered, sems = scratch
    slab = field.shape[0]
    got = load([(lookup, table), (conductance, weight)], sems)
    fill_own(extended, field)
    fill_rim(extended, first[:slab], second[:slab])
    for copy in got:
        copy.wait()
    local = apply[:slab, :slab]
    for piece, values in conducted(table, weight, mask, spread, extended, gathered, chunks(field.shape[1])):
        out[:, piece] = values + axial_step * mask[:, piece] * product(local, flux[:, piece])


def last_kernel(spans, base, mask, apply, *refs):
    got, (out,) = refs[: spans - 1], refs[spans - 1 :]
    slab = base.shape[0]
    weights = apply[:slab, slab:]
    for piece in chunks(base.shape[1]):
        out[:, piece] = base[:, piece] + axial_step * mask[:, piece] * product(weights, stacked(got, piece))


def in_place(array):
    return pltpu.with_memory_space_constraint(array, pltpu.HBM)


def call(kernel, far, near, shapes, scratch=(), flops=0, name=None):
    size = sum(4 * math.prod(shape) for shape in shapes) + sum(4 * a.size for a in near)
    return pl.pallas_call(
        kernel,
        in_specs=[pl.BlockSpec(memory_space=pltpu.HBM)] * len(far) + [pl.BlockSpec(memory_space=pltpu.VMEM)] * len(near),
        out_specs=[pl.BlockSpec(memory_space=pltpu.VMEM)] * len(shapes),
        out_shape=[jax.ShapeDtypeStruct(shape, jnp.float32) for shape in shapes],
        scratch_shapes=list(scratch),
        compiler_params=pltpu.CompilerParams(vmem_limit_bytes=24 * 2**20),
        cost_estimate=pl.CostEstimate(flops=flops, bytes_accessed=size, transcendentals=0),
        name=name,
    )(*[in_place(array) for array in far], *near)


def trade_faces(first, second):
    count = lax.axis_size("xs")
    swap = lambda start: [pair for i in range(start, count - 1, 2) for pair in ((i, i + 1), (i + 1, i))]
    return lax.ppermute(first, "xs", swap(0)), lax.ppermute(second, "xs", swap(1))


def trade_slabs(parts):
    count = lax.axis_size("hgt")
    return [lax.ppermute(part, "hgt", [(i, i ^ x) for i in range(count)]) for x, part in enumerate(parts, 1)]


def slab_body(factors, field, kappa, lookup, conductance, exported, totals, pipe, matrix):
    slab, nodes = field.shape
    spans = lax.axis_size("hgt")
    ranks = factors["ranks"]
    rows = sum(ranks)
    faces = exported.shape[1:]
    rim = faces[1] * matrix.shape[0]
    tables = [lookup.T, conductance.T]
    exported = exported.reshape(faces)
    tall = slab + carried_rows
    tiles = (nodes + 2 * rim) // lanes + 1
    sent = [(rank, nodes) for rank in ranks]
    whole = (slab, nodes)
    work = 2 * nodes * slab * slab

    def conduct_scratch(height):
        return [
            pltpu.SMEM(tables[0].shape, jnp.int32),
            pltpu.SMEM(tables[1].shape, jnp.float32),
            pltpu.VMEM((2, tiles, height, lanes), jnp.float32),
            pltpu.VMEM((height, nodes), jnp.float32),
            pltpu.SemaphoreType.DMA((2,)),
        ]

    face_scratch = pltpu.SMEM(faces, jnp.int32)
    first, second = call(
        faces_kernel,
        [exported, field],
        [],
        [(slab, rim)] * 2,
        [face_scratch, pltpu.VMEM((slab, nodes // 2), jnp.float32), pltpu.SemaphoreType.DMA((2,))],
        name="faces",
    )
    left, right = trade_faces(first, second)
    stacks = [factors[key] for key in ("send_first", "send_joint", "apply_first", "apply_joint", "apply_carried")]
    sizes = [stack.shape[1:] for stack in stacks]
    mask, spread, state, moments, send_first, send_joint, apply_first, apply_joint, onward = pl.pallas_call(
        functools.partial(prepare_kernel, sizes),
        in_specs=[pl.BlockSpec(memory_space=pltpu.SMEM)]
        + [pl.BlockSpec(memory_space=pltpu.VMEM)] * 3
        + [pl.BlockSpec(memory_space=pltpu.HBM)] * len(stacks),
        out_specs=[pl.BlockSpec(memory_space=pltpu.VMEM)] * (4 + len(stacks)),
        out_shape=[
            jax.ShapeDtypeStruct(shape, jnp.float32)
            for shape in [(1, nodes), (2 * lanes, 2 * lanes), whole, (rows, nodes)] + sizes
        ],
        scratch_shapes=[pltpu.SemaphoreType.DMA((len(stacks),))],
        compiler_params=pltpu.CompilerParams(vmem_limit_bytes=24 * 2**20),
        cost_estimate=pl.CostEstimate(flops=work, bytes_accessed=4 * slab * nodes, transcendentals=0),
        name="prepare",
    )(totals, pipe.reshape(1, nodes), matrix, field, *[in_place(stack) for stack in stacks])
    parts = call(
        moments_kernel, tables, [moments, left, right, mask, spread, send_first], sent, conduct_scratch(rows), name="moments"
    )
    parts = trade_slabs(parts)
    state, slope = call(
        first_kernel,
        tables,
        [state, left, right, mask, spread, apply_first],
        [whole, whole],
        conduct_scratch(slab),
        2 * work,
        name="first",
    )
    flux, carried, *joint = call(
        functools.partial(flux_kernel, spans),
        [],
        [slope, *parts, kappa, apply_first, send_joint],
        [whole, (carried_rows, nodes)] + sent,
        name="flux",
    )
    joint = trade_slabs(joint)
    (base,) = call(local_kernel, [], [state, carried, flux, mask, apply_joint], [(tall, nodes)], flops=work, name="local")
    first, second = call(
        functools.partial(rim_kernel, spans),
        [exported],
        [base, mask, apply_joint, *joint],
        [(tall, rim)] * 2,
        [face_scratch, pltpu.SemaphoreType.DMA((1,))],
        name="rim",
    )
    left, right = trade_faces(first, second)
    state, slope = call(
        functools.partial(close_kernel, spans), [], [base, mask, apply_joint, onward, *joint], [whole, whole], flops=work, name="close"
    )
    flux, *parts = call(
        second_kernel,
        tables,
        [slope, left, right, mask, spread, kappa, onward, send_first],
        [whole] + sent,
        conduct_scratch(slab),
        name="second",
    )
    parts = trade_slabs(parts)
    (base,) = call(
        rest_kernel,
        tables,
        [state, flux, left, right, mask, spread, apply_first],
        [whole],
        conduct_scratch(slab),
        2 * work,
        name="rest",
    )
    (state,) = call(functools.partial(last_kernel, spans), [], [base, mask, apply_first, *parts], [whole], name="last")
    return state


def padded_2(cells, sides, width):
    for axis, dim in sides:
        count = lax.axis_size(axis)
        ends = count - 1
        head = lax.slice_in_dim(cells, 0, width, axis=dim)
        tail = lax.slice_in_dim(cells, cells.shape[dim] - width, cells.shape[dim], axis=dim)
        cells = jnp.concatenate(
            [
                lax.ppermute(tail, axis, [(i, (i + 1) % count) for i in range(ends)]),
                cells,
                lax.ppermute(head, axis, [((i + 1) % count, i) for i in range(ends)]),
            ],
            axis=dim,
        )
    return cells


def cheb_matrix(order):
    index = jnp.arange(order)
    row_f = index[:, None].astype(jnp.float32)
    col_f = index[None, :].astype(jnp.float32)
    angle = math.pi / (2.0 * (order - 1))
    difference = -2.0 * jnp.sin((row_f + col_f) * angle) * jnp.sin((row_f - col_f) * angle)
    ends = (index == 0) | (index == order - 1)
    weight = jnp.where(ends, 2.0, 1.0).astype(jnp.float32)
    parity = jnp.where((index[:, None] + index[None, :]) % 2 == 0, 1.0, -1.0).astype(jnp.float32)
    off_diag = index[:, None] != index[None, :]
    safe_diff = jnp.where(off_diag, difference, jnp.float32(1.0))
    entries = jnp.where(
        off_diag, weight[:, None] / weight[None, :] * parity / safe_diff, jnp.float32(0.0)
    )
    entries = entries - jnp.diag(jnp.sum(entries, axis=1))
    mirror = jnp.minimum(index, order - 1 - index).astype(jnp.float32)
    sine = jnp.sin(mirror * (2.0 * angle))
    return -sine[:, None] * entries / (order - 1)


def slot_sum(source, indices, boundary_entry_conductances, total):
    for slot_index in range(indices.shape[1]):
        picked = source[:, indices[:, slot_index], :]
        total = total + boundary_entry_conductances[None, :, slot_index, None] * picked
    return total


def conduct(
    present_solution,
    boundary_group_lookup,
    boundary_entry_conductances,
    exported_boundary_groups,
    spread,
    slab_mask,
    width,
):
    height, plane_vertices = present_solution.shape
    blocks = plane_vertices // width
    face_count = exported_boundary_groups.shape[2]
    blocked = present_solution.reshape(height, blocks, width)
    outgoing = jnp.concatenate(
        [
            blocked[:, exported_boundary_groups[0, 0], :],
            blocked[:, exported_boundary_groups[0, 1], :],
        ],
        axis=1,
    )
    outgoing = outgoing.reshape(height, 2 * face_count * width)
    rim_width = face_count * width
    padded = padded_2(outgoing, (("xs", 1),), rim_width)
    from_left = padded[:, :rim_width].reshape(height, face_count, width)
    from_right = padded[:, padded.shape[1] - rim_width :].reshape(height, face_count, width)
    empty = jnp.zeros((height, 1, width), jnp.float32)
    gathered = jnp.zeros((height, blocks, width), jnp.float32)
    extended = jnp.concatenate([blocked, from_left, from_right, empty], axis=1)
    gathered = slot_sum(extended, boundary_group_lookup, boundary_entry_conductances, gathered)
    coupled = jnp.dot(
        gathered.reshape(-1, spread.shape[0]),
        spread,
        precision=lax.Precision.HIGHEST,
        preferred_element_type=jnp.float32,
    ).reshape(height, plane_vertices)
    return present_solution + slab_mask[None, :] * coupled


def axial(column_field, column_kappa, operator, column_mask):
    slope = jnp.dot(
        operator, column_field, precision=lax.Precision.HIGHEST, preferred_element_type=jnp.float32
    )
    second = jnp.dot(
        operator,
        column_kappa * slope,
        precision=lax.Precision.HIGHEST,
        preferred_element_type=jnp.float32,
    )
    return column_field + axial_step * column_mask[None, :] * second


def to_columns(moved):
    return lax.all_to_all(moved, "hgt", split_axis=1, concat_axis=0, tiled=True)


def to_slabs(result):
    return lax.all_to_all(result, "hgt", split_axis=0, concat_axis=1, tiled=True)


def column_body(
    thermal_field,
    thermal_diffusivity,
    boundary_group_lookup,
    boundary_entry_conductances,
    exported_boundary_groups,
    domain_group_totals,
    pipe_cavity_indicator,
    boundary_vertex_matrix,
):
    layer_sample_number, plane_vertices = thermal_field.shape
    width = boundary_vertex_matrix.shape[0]
    group_size = max(1, 128 // width)
    spread = jnp.kron(jnp.eye(group_size, dtype=jnp.float32), boundary_vertex_matrix)
    block_ids = jnp.arange(plane_vertices) // width
    live_groups = block_ids < domain_group_totals[0]
    slab_mask = jnp.where(live_groups & (pipe_cavity_indicator == 0), 1.0, 0.0).astype(jnp.float32)
    spans = lax.axis_size("hgt")
    column_count = plane_vertices // spans
    column_start = lax.axis_index("hgt") * column_count
    column_mask = lax.dynamic_slice_in_dim(slab_mask, column_start, column_count, 0)
    operator = cheb_matrix(layer_sample_number * spans)
    present_solution = jnp.where(live_groups[None, :], thermal_field, jnp.float32(0.0))
    moved = conduct(
        present_solution,
        boundary_group_lookup,
        boundary_entry_conductances,
        exported_boundary_groups,
        spread,
        slab_mask,
        width,
    )
    column_field, kappa_fixed = (
        lax.all_to_all(moved, "hgt", split_axis=1, concat_axis=0, tiled=True),
        lax.all_to_all(thermal_diffusivity, "hgt", split_axis=1, concat_axis=0, tiled=True),
    )
    result = axial(column_field, kappa_fixed, operator, column_mask)
    present_solution = to_slabs(result)
    moved = conduct(
        present_solution,
        boundary_group_lookup,
        boundary_entry_conductances,
        exported_boundary_groups,
        spread,
        slab_mask,
        width,
    )
    result = axial(to_columns(moved), kappa_fixed, operator, column_mask)
    present_solution = to_slabs(result)
    return present_solution


def body(field, kappa, lookup, conductance, exported, totals, pipe, matrix):
    spans = lax.axis_size("hgt")
    factors = slab_factors(field.shape[0] * spans, spans)
    args = (field, kappa, lookup, conductance, exported, totals, pipe, matrix)
    if factors is None or 2 * matrix.shape[0] != lanes:
        return column_body(*args)
    return slab_body(factors, *args)


def solution(mesh):
    in_specs = (
        P("hgt", ("grp", "xs")),
        P("hgt", ("grp", "xs")),
        P("xs", None),
        P("xs", None),
        P("xs", None, None),
        P("xs"),
        P("xs"),
        P(),
    )
    out_specs = P("hgt", ("grp", "xs"))
    return jax.shard_map(body, mesh=mesh, in_specs=in_specs, out_specs=out_specs, check_vma=False)
```

```python
import functools
import math

import ml_dtypes
import numpy as np
import jax
import jax.numpy as jnp
from jax import lax
from jax.experimental import pallas as pl
from jax.experimental.pallas import tpu as pltpu
from jax.sharding import PartitionSpec as P

axial_step = 0.5
lanes = 128
near_rows = 12
far_rows = 4
joint_near_rows = 16
joint_far_rows = 8
carried_rows = 24


def cheb_exact(order):
    index = np.arange(order, dtype=np.float64)
    angle = math.pi / (2.0 * (order - 1))
    row, col = index[:, None], index[None, :]
    difference = -2.0 * np.sin((row + col) * angle) * np.sin((row - col) * angle)
    weight = np.ones(order)
    weight[0] = weight[-1] = 2.0
    parity = np.where((row + col) % 2 == 0, 1.0, -1.0)
    off_diag = row != col
    entries = np.where(
        off_diag, weight[:, None] / weight[None, :] * parity / np.where(off_diag, difference, 1.0), 0.0
    )
    entries = entries - np.diag(entries.sum(axis=1))
    sine = np.sin(np.minimum(index, order - 1 - index) * (2.0 * angle))
    return -sine[:, None] * entries / (order - 1)


def row_basis(block, rank):
    return np.linalg.svd(block, full_matrices=False)[2][:rank]


def halves(matrix):
    high = matrix.astype(ml_dtypes.bfloat16)
    return high, (matrix - high.astype(np.float64)).astype(ml_dtypes.bfloat16)


def pad_to(matrix, rows, cols):
    return np.pad(matrix, ((0, rows - matrix.shape[0]), (0, cols - matrix.shape[1])))


def round_up(size, step):
    return -(-size // step) * step


def as_left(matrix):
    high, low = halves(pad_to(matrix, matrix.shape[0], round_up(matrix.shape[1], 16)))
    return np.concatenate([high, high, low], axis=1)


def fold(rows, half, axis):
    whole = rows.shape[axis] // 8 * 8
    head, tail = np.split(rows, [whole], axis=axis)
    if not tail.shape[axis]:
        return head, tail
    zeros = np.zeros_like(tail)
    return head, np.concatenate([zeros, tail] if half else [tail, zeros], axis=axis)


def folded(parts, half, axis):
    pairs = [fold(part, half, axis) for part in parts]
    return np.concatenate([head for head, _ in pairs] + [tail for _, tail in pairs], axis=axis)


@functools.lru_cache(maxsize=None)
def slab_factors(order, spans):
    slab = order // spans
    if spans & (spans - 1) or spans > 4 or slab < 128:
        return None
    full = cheb_exact(order)
    block = lambda s, t: full[s * slab : (s + 1) * slab, t * slab : (t + 1) * slab]
    near = [any(abs(s - (s ^ x)) == 1 for s in range(spans)) for x in range(1, spans)]
    ranks = [near_rows if close else far_rows for close in near]
    joint_ranks = [joint_near_rows if close else joint_far_rows for close in near]
    first, joint = {}, {}
    carried, onward, left = {}, {}, {}
    for s in range(spans):
        others = [t for t in range(spans) if t != s]
        u, sigma, vt = np.linalg.svd(np.concatenate([block(s, t) for t in others], axis=1), full_matrices=False)
        left[s] = u[:, :carried_rows]
        rows = sigma[:carried_rows, None] * vt[:carried_rows]
        carried[s] = {t: rows[:, i * slab : (i + 1) * slab] for i, t in enumerate(others)}
        onward[s] = sum(carried[s][t] @ full[t * slab : (t + 1) * slab] for t in others)
        for t in others:
            first[s, t] = row_basis(block(s, t), ranks[(s ^ t) - 1])
            joint[s, t] = row_basis(
                np.concatenate([block(s, t), onward[s][:, t * slab : (t + 1) * slab]], axis=0), joint_ranks[(s ^ t) - 1]
            )
    sets = {}

    def add(name, matrix):
        sets.setdefault(name, []).append(as_left(matrix))

    for s in range(spans):
        partners = [s ^ x for x in range(1, spans)]
        cut = lambda t: slice(t * slab, (t + 1) * slab)
        firsts = [np.concatenate([block(s, t), carried[s][t]], axis=0) @ first[s, t].T for t in partners]
        joints = [np.concatenate([block(s, t), onward[s][:, cut(t)]], axis=0) @ joint[s, t].T for t in partners]
        for half in range(2):
            add("send_half%d" % half, folded([first[t, s] for t in partners], half, 0))
            add("far_half%d" % half, folded(firsts, half, 1))
        add("send_rows", folded([first[t, s] for t in partners], 0, 0))
        add("send_joint", np.concatenate([joint[t, s] for t in partners], axis=0))
        add("far_joint", np.concatenate(joints, axis=1))
        add("local", np.concatenate([block(s, s), onward[s][:, cut(s)]], axis=0))
        add("onward", np.concatenate([block(s, s), left[s]], axis=1))
    return dict(
        ranks=ranks, joint_ranks=joint_ranks, sets={name: np.stack(parts) for name, parts in sets.items()}
    )


def split(values):
    high = values.astype(jnp.bfloat16)
    return high, (values - high.astype(jnp.float32)).astype(jnp.bfloat16)


def left_product(left, values):
    short = left.shape[1] // 3 - values.shape[0]
    if short:
        values = jnp.concatenate([values, jnp.zeros((short, values.shape[1]), jnp.float32)], axis=0)
    high, low = split(values)
    return jnp.dot(left, jnp.concatenate([high, low, high], axis=0), preferred_element_type=jnp.float32)


def right_product(values, right):
    high, low = split(values)
    return jnp.dot(jnp.concatenate([high, low, high], axis=1), right, preferred_element_type=jnp.float32)


def low_half():
    return lax.broadcasted_iota(jnp.int32, (1, lanes), 1) < lanes // 2


def tile_at(tile):
    return slice(tile * lanes, (tile + 1) * lanes)


def chunks(width):
    step = min(width, 512)
    return [slice(start, start + step) for start in range(0, width, step)]


def load(copies, sems):
    started = [pltpu.make_async_copy(source, target, sems.at[i]) for i, (source, target) in enumerate(copies)]
    for copy in started:
        copy.start()
    return started


def sides():
    first = 1 - lax.axis_index("xs") % 2
    return first, 1 - first


def take_face(source, exported, side):
    tiles = []
    for tile in range(exported.shape[1] // 2):
        parts = []
        for place in range(2):
            index = exported[side, 2 * tile + place]
            value = source[:, pl.ds(pl.multiple_of(index // 2 * lanes, lanes), lanes)]
            parts.append(jnp.where(index % 2 == place, value, pltpu.roll(value, lanes // 2, 1)))
        tiles.append(jnp.where(low_half(), parts[0], parts[1]))
    return jnp.concatenate(tiles, axis=1)


def faces_kernel(exported, field, first, second, faces, near, sems):
    got = load([(exported, faces), (field.at[:, pl.ds(0, near.shape[1])], near)], sems)
    for copy in got:
        copy.wait()
    for side, out in zip(sides(), (first, second)):
        out[...] = take_face(near, faces, side)


def prepare_kernel(count, total, pipe, matrix, field, *refs):
    stacks, (mask, spread, state, moments), outs = refs[:count], refs[count : count + 4], refs[count + 4 : 2 * count + 4]
    holes, block_matrix, values, sems = refs[2 * count + 4 :]
    where = lax.axis_index("hgt")
    pairs = [(matrix, block_matrix), (pipe, holes), (field, values)]
    got = load(pairs + [(stack.at[where], out) for stack, out in zip(stacks, outs)], sems)
    got[0].wait()
    width = matrix.shape[0]
    size = spread.shape[1]
    wide = jnp.concatenate([block_matrix[...]] * (size // width), axis=1)
    tall = jnp.concatenate([wide] * (size // width), axis=0)
    row = lax.broadcasted_iota(jnp.int32, tall.shape, 0) // width
    col = lax.broadcasted_iota(jnp.int32, tall.shape, 1) // width
    high, low = split(jnp.where(row == col, tall, 0.0))
    spread[...] = jnp.concatenate([high, high, low], axis=0)
    got[1].wait()
    block = lax.broadcasted_iota(jnp.int32, mask.shape, 1) // width
    live = block < total[0]
    mask[...] = jnp.where(live & (holes[...] == 0), 1.0, 0.0).astype(jnp.float32)
    for copy in got[2:]:
        copy.wait()
    for piece in chunks(field.shape[1]):
        state[:, piece] = jnp.where(live[:, piece], values[:, piece], 0.0)
        moments[:, piece] = left_product(outs[0][...], state[:, piece])


def fill(extended, tile, value):
    extended[0, tile] = value
    extended[1, tile] = pltpu.roll(value, lanes // 2, 1)


def fill_own(extended, own):
    tiles = own.shape[1] // lanes
    for tile in range(tiles):
        fill(extended, tile, own[:, tile_at(tile)])
    fill(extended, extended.shape[1] - 1, jnp.zeros(extended.shape[2:], jnp.float32))


def fill_rim(extended, first, second):
    rim = first.shape[1] // lanes
    start = extended.shape[1] - 1 - 2 * rim
    for side, values in zip(sides(), (first, second)):
        for tile in range(rim):
            fill(extended, start + side * rim + tile, values[:, tile_at(tile)])


def conducted(lookup, conductance, mask, spread, extended, gathered, pieces):
    half = low_half()
    per = spread.shape[1] // lanes
    for piece in pieces:
        start = piece.start // lanes
        for tile in range(start, piece.stop // lanes):
            low, high = 2 * tile, 2 * tile + 1
            total = jnp.where(half, conductance[0, low], conductance[0, high]) * extended[0, tile]
            for slot in range(1, lookup.shape[0]):
                one, two = lookup[slot, low], lookup[slot, high]
                value = jnp.where(half, extended[one % 2, one // 2], extended[1 - two % 2, two // 2])
                total = total + jnp.where(half, conductance[slot, low], conductance[slot, high]) * value
            gathered[:, tile_at(tile)] = total
        moved = []
        for tile in range(start, piece.stop // lanes, per):
            part = slice(tile * lanes, (tile + per) * lanes)
            own = jnp.concatenate([extended[0, tile + i] for i in range(per)], axis=1)
            moved.append(own + mask[:, part] * right_product(gathered[:, part], spread[...]))
        yield piece, jnp.concatenate(moved, axis=1)


def store_rows(moved, outs, piece):
    start = 0
    for out in outs:
        out[:, piece] = moved[start : start + out.shape[0]]
        start += out.shape[0]


def stacked(refs, piece):
    return jnp.concatenate([ref[:, piece] for ref in refs], axis=0)


def folded_views(refs, piece, nodes):
    half = piece.start // (nodes // 2)
    heads = [(ref, piece) for ref in refs if ref.shape[1] >= nodes]
    tails = []
    for ref in refs:
        start = (nodes if ref.shape[1] >= nodes else 0) + piece.start - half * (nodes // 2)
        if ref.shape[1] != nodes:
            tails.append((ref, slice(start, start + piece.stop - piece.start)))
    return half, heads, tails


def store_folded(moved, refs, piece, nodes):
    half, heads, tails = folded_views(refs, piece, nodes)
    for i, (ref, part) in enumerate(heads + tails):
        value = moved[8 * i : 8 * i + 8]
        ref[:, part] = ref[:, part] + value if half and i >= len(heads) else value


def load_folded(refs, piece, nodes):
    half, heads, tails = folded_views(refs, piece, nodes)
    return half, jnp.concatenate([ref[:, part] for ref, part in heads + tails], axis=0)


def moments_kernel(lookup, conductance, moments, first, second, mask, spread, send, *refs):
    outs, (table, weight, extended, gathered, sems) = refs[:-5], refs[-5:]
    nodes = moments.shape[1]
    got = load([(lookup, table), (conductance, weight)], sems)
    fill_own(extended, moments)
    fill_rim(extended, left_product(send[...], first[...]), left_product(send[...], second[...]))
    for copy in got:
        copy.wait()
    whole = 8 * sum(out.shape[1] >= nodes for out in outs)
    for piece, values in conducted(table, weight, mask, spread, extended, gathered, chunks(nodes)):
        if piece.start >= nodes // 2:
            tails = [pltpu.roll(values[i : i + 8], 4, 0) for i in range(whole, values.shape[0], 8)]
            values = jnp.concatenate([values[:whole]] + tails, axis=0)
        store_folded(values, outs, piece, nodes)


def first_kernel(lookup, conductance, field, first, second, mask, spread, local, out, slope, *scratch):
    table, weight, extended, gathered, sems = scratch
    slab = field.shape[0]
    got = load([(lookup, table), (conductance, weight)], sems)
    fill_own(extended, field)
    fill_rim(extended, first, second)
    for copy in got:
        copy.wait()
    for piece, values in conducted(table, weight, mask, spread, extended, gathered, chunks(field.shape[1])):
        out[:, piece] = values
        slope[:, piece] = left_product(local[:slab], values)


def flux_kernel(spans, slope, *refs):
    got, (kappa, send), fars, (flux, carried), outs = (
        refs[: spans - 1],
        refs[spans - 1 : spans + 1],
        refs[spans + 1 : spans + 3],
        refs[spans + 3 : spans + 5],
        refs[spans + 5 :],
    )
    slab, nodes = slope.shape
    for piece in chunks(nodes):
        half, rows = load_folded(got, piece, nodes)
        far = left_product(fars[half][...], rows)
        carried[:, piece] = far[slab:]
        value = kappa[:, piece] * (slope[:, piece] + far[:slab])
        flux[:, piece] = value
        store_rows(left_product(send[...], value), outs, piece)


def local_kernel(field, carried, flux, mask, local, out):
    slab = field.shape[0]
    for piece in chunks(field.shape[1]):
        step = axial_step * mask[:, piece] * left_product(local[...], flux[:, piece])
        out[:slab, piece] = field[:, piece] + step[:slab]
        out[slab:, piece] = carried[:, piece] + step[slab:]


def rim_kernel(spans, exported, base, mask, far, *refs):
    got, (first, second, faces, sems) = refs[: spans - 1], refs[spans - 1 :]
    (copy,) = load([(exported, faces)], sems)
    copy.wait()
    for side, out in zip(sides(), (first, second)):
        rows = jnp.concatenate([take_face(ref, faces, side) for ref in got], axis=0)
        out[...] = take_face(base, faces, side) + axial_step * take_face(mask, faces, side) * left_product(far[...], rows)


def close_kernel(spans, base, mask, far, onward, *refs):
    got, (out, slope) = refs[: spans - 1], refs[spans - 1 :]
    slab = out.shape[0]
    for piece in chunks(base.shape[1]):
        values = base[:, piece] + axial_step * mask[:, piece] * left_product(far[...], stacked(got, piece))
        out[:, piece] = values[:slab]
        slope[:, piece] = left_product(onward[...], values)


def second_kernel(lookup, conductance, slope, first, second, mask, spread, kappa, onward, *refs):
    sends, flux, outs, (table, weight, extended, gathered, sems) = refs[:2], refs[2], refs[3:-5], refs[-5:]
    nodes = slope.shape[1]
    got = load([(lookup, table), (conductance, weight)], sems)
    fill_own(extended, slope)
    fill_rim(extended, left_product(onward[...], first[...]), left_product(onward[...], second[...]))
    for copy in got:
        copy.wait()
    for piece, values in conducted(table, weight, mask, spread, extended, gathered, chunks(nodes)):
        value = kappa[:, piece] * values
        flux[:, piece] = value
        half = piece.start // (nodes // 2)
        store_folded(left_product(sends[half][...], value), outs, piece, nodes)


def rest_kernel(lookup, conductance, field, flux, first, second, mask, spread, local, out, *scratch):
    table, weight, extended, gathered, sems = scratch
    slab = field.shape[0]
    got = load([(lookup, table), (conductance, weight)], sems)
    fill_own(extended, field)
    fill_rim(extended, first[:slab], second[:slab])
    for copy in got:
        copy.wait()
    for piece, values in conducted(table, weight, mask, spread, extended, gathered, chunks(field.shape[1])):
        out[:, piece] = values + axial_step * mask[:, piece] * left_product(local[:slab], flux[:, piece])


def last_kernel(spans, base, mask, *refs):
    fars, got, (out,) = refs[:2], refs[2 : spans + 1], refs[spans + 1 :]
    slab, nodes = base.shape
    for piece in chunks(nodes):
        half, rows = load_folded(got, piece, nodes)
        out[:, piece] = base[:, piece] + axial_step * mask[:, piece] * left_product(fars[half][:slab], rows)


def in_place(array):
    return pltpu.with_memory_space_constraint(array, pltpu.HBM)


def call(kernel, far, near, outs, scratch=(), flops=0, name=None, scalars=()):
    outs = [out if isinstance(out, jax.ShapeDtypeStruct) else jax.ShapeDtypeStruct(out, jnp.float32) for out in outs]
    size = sum(4 * array.size for array in [*near, *outs])
    spaces = [(scalars, pltpu.SMEM), (far, pltpu.HBM), (near, pltpu.VMEM)]
    return pl.pallas_call(
        kernel,
        in_specs=[pl.BlockSpec(memory_space=space) for arrays, space in spaces for _ in arrays],
        out_specs=[pl.BlockSpec(memory_space=pltpu.VMEM)] * len(outs),
        out_shape=outs,
        scratch_shapes=list(scratch),
        compiler_params=pltpu.CompilerParams(vmem_limit_bytes=24 * 2**20),
        cost_estimate=pl.CostEstimate(flops=flops, bytes_accessed=size, transcendentals=0),
        name=name,
    )(*scalars, *[in_place(array) for array in far], *near)


def trade_faces(first, second):
    count = lax.axis_size("xs")
    swap = lambda start: [pair for i in range(start, count - 1, 2) for pair in ((i, i + 1), (i + 1, i))]
    return lax.ppermute(first, "xs", swap(0)), lax.ppermute(second, "xs", swap(1))


def trade_slabs(parts):
    count = lax.axis_size("hgt")
    return [lax.ppermute(part, "hgt", [(i, i ^ x) for i in range(count)]) for x, part in enumerate(parts, 1)]


def slab_body(factors, field, kappa, lookup, conductance, exported, totals, pipe, matrix):
    slab, nodes = field.shape
    spans = lax.axis_size("hgt")
    faces = exported.shape[1:]
    rim = faces[1] * matrix.shape[0]
    tables = [lookup.T, conductance.T]
    exported = exported.reshape(faces)
    tall = slab + carried_rows
    tiles = (nodes + 2 * rim) // lanes + 1
    sent = [(8, rank // 8 * nodes + (rank % 8 > 0) * nodes // 2) for rank in factors["ranks"]]
    sent_joint = [(rank, nodes) for rank in factors["joint_ranks"]]
    whole = (slab, nodes)
    work = 2 * nodes * slab * slab

    def conduct_scratch(height):
        return [
            pltpu.SMEM(tables[0].shape, jnp.int32),
            pltpu.SMEM(tables[1].shape, jnp.float32),
            pltpu.VMEM((2, tiles, height, lanes), jnp.float32),
            pltpu.VMEM((height, nodes), jnp.float32),
            pltpu.SemaphoreType.DMA((2,)),
        ]

    face_scratch = pltpu.SMEM(faces, jnp.int32)
    first, second = call(
        faces_kernel,
        [exported, field],
        [],
        [(slab, rim)] * 2,
        [face_scratch, pltpu.VMEM((slab, nodes // 2), jnp.float32), pltpu.SemaphoreType.DMA((2,))],
        name="faces",
    )
    left, right = trade_faces(first, second)
    names = ["send_rows"] + sorted(name for name in factors["sets"] if name != "send_rows")
    stacks = [jnp.asarray(factors["sets"][name]) for name in names]
    height = stacks[0].shape[1]
    spread = jax.ShapeDtypeStruct((6 * lanes, 2 * lanes), jnp.bfloat16)
    mask, spread, state, moments, *own = call(
        functools.partial(prepare_kernel, len(stacks)),
        [pipe.reshape(1, nodes), matrix, field, *stacks],
        [],
        [(1, nodes), spread, whole, (height, nodes)]
        + [jax.ShapeDtypeStruct(stack.shape[1:], jnp.bfloat16) for stack in stacks],
        [
            pltpu.VMEM((1, nodes), jnp.int32),
            pltpu.VMEM(matrix.shape, jnp.float32),
            pltpu.VMEM(whole, jnp.float32),
            pltpu.SemaphoreType.DMA((3 + len(stacks),)),
        ],
        work,
        "prepare",
        [totals],
    )
    own = dict(zip(names, own))
    sends = [own["send_half0"], own["send_half1"]]
    fars = [own["far_half0"], own["far_half1"]]
    parts = call(
        moments_kernel, tables, [moments, left, right, mask, spread, own["send_rows"]], sent, conduct_scratch(height), name="moments"
    )
    parts = trade_slabs(parts)
    state, slope = call(
        first_kernel,
        tables,
        [state, left, right, mask, spread, own["local"]],
        [whole, whole],
        conduct_scratch(slab),
        2 * work,
        "first",
    )
    flux, carried, *joint = call(
        functools.partial(flux_kernel, spans),
        [],
        [slope, *parts, kappa, own["send_joint"], *fars],
        [whole, (carried_rows, nodes)] + sent_joint,
        name="flux",
    )
    joint = trade_slabs(joint)
    (base,) = call(local_kernel, [], [state, carried, flux, mask, own["local"]], [(tall, nodes)], flops=work, name="local")
    first, second = call(
        functools.partial(rim_kernel, spans),
        [exported],
        [base, mask, own["far_joint"], *joint],
        [(tall, rim)] * 2,
        [face_scratch, pltpu.SemaphoreType.DMA((1,))],
        name="rim",
    )
    left, right = trade_faces(first, second)
    state, slope = call(
        functools.partial(close_kernel, spans),
        [],
        [base, mask, own["far_joint"], own["onward"], *joint],
        [whole, whole],
        flops=work,
        name="close",
    )
    flux, *parts = call(
        second_kernel,
        tables,
        [slope, left, right, mask, spread, kappa, own["onward"], *sends],
        [whole] + sent,
        conduct_scratch(slab),
        name="second",
    )
    parts = trade_slabs(parts)
    (base,) = call(
        rest_kernel,
        tables,
        [state, flux, left, right, mask, spread, own["local"]],
        [whole],
        conduct_scratch(slab),
        2 * work,
        "rest",
    )
    (state,) = call(functools.partial(last_kernel, spans), [], [base, mask, *fars, *parts], [whole], name="last")
    return state


def padded_2(cells, sides, width):
    for axis, dim in sides:
        count = lax.axis_size(axis)
        ends = count - 1
        head = lax.slice_in_dim(cells, 0, width, axis=dim)
        tail = lax.slice_in_dim(cells, cells.shape[dim] - width, cells.shape[dim], axis=dim)
        cells = jnp.concatenate(
            [
                lax.ppermute(tail, axis, [(i, (i + 1) % count) for i in range(ends)]),
                cells,
                lax.ppermute(head, axis, [((i + 1) % count, i) for i in range(ends)]),
            ],
            axis=dim,
        )
    return cells


def cheb_matrix(order):
    index = jnp.arange(order)
    row_f = index[:, None].astype(jnp.float32)
    col_f = index[None, :].astype(jnp.float32)
    angle = math.pi / (2.0 * (order - 1))
    difference = -2.0 * jnp.sin((row_f + col_f) * angle) * jnp.sin((row_f - col_f) * angle)
    ends = (index == 0) | (index == order - 1)
    weight = jnp.where(ends, 2.0, 1.0).astype(jnp.float32)
    parity = jnp.where((index[:, None] + index[None, :]) % 2 == 0, 1.0, -1.0).astype(jnp.float32)
    off_diag = index[:, None] != index[None, :]
    safe_diff = jnp.where(off_diag, difference, jnp.float32(1.0))
    entries = jnp.where(
        off_diag, weight[:, None] / weight[None, :] * parity / safe_diff, jnp.float32(0.0)
    )
    entries = entries - jnp.diag(jnp.sum(entries, axis=1))
    mirror = jnp.minimum(index, order - 1 - index).astype(jnp.float32)
    sine = jnp.sin(mirror * (2.0 * angle))
    return -sine[:, None] * entries / (order - 1)


def slot_sum(source, indices, boundary_entry_conductances, total):
    for slot_index in range(indices.shape[1]):
        picked = source[:, indices[:, slot_index], :]
        total = total + boundary_entry_conductances[None, :, slot_index, None] * picked
    return total


def conduct(
    present_solution,
    boundary_group_lookup,
    boundary_entry_conductances,
    exported_boundary_groups,
    spread,
    slab_mask,
    width,
):
    height, plane_vertices = present_solution.shape
    blocks = plane_vertices // width
    face_count = exported_boundary_groups.shape[2]
    blocked = present_solution.reshape(height, blocks, width)
    outgoing = jnp.concatenate(
        [
            blocked[:, exported_boundary_groups[0, 0], :],
            blocked[:, exported_boundary_groups[0, 1], :],
        ],
        axis=1,
    )
    outgoing = outgoing.reshape(height, 2 * face_count * width)
    rim_width = face_count * width
    padded = padded_2(outgoing, (("xs", 1),), rim_width)
    from_left = padded[:, :rim_width].reshape(height, face_count, width)
    from_right = padded[:, padded.shape[1] - rim_width :].reshape(height, face_count, width)
    empty = jnp.zeros((height, 1, width), jnp.float32)
    gathered = jnp.zeros((height, blocks, width), jnp.float32)
    extended = jnp.concatenate([blocked, from_left, from_right, empty], axis=1)
    gathered = slot_sum(extended, boundary_group_lookup, boundary_entry_conductances, gathered)
    coupled = jnp.dot(
        gathered.reshape(-1, spread.shape[0]),
        spread,
        precision=lax.Precision.HIGHEST,
        preferred_element_type=jnp.float32,
    ).reshape(height, plane_vertices)
    return present_solution + slab_mask[None, :] * coupled


def axial(column_field, column_kappa, operator, column_mask):
    slope = jnp.dot(
        operator, column_field, precision=lax.Precision.HIGHEST, preferred_element_type=jnp.float32
    )
    second = jnp.dot(
        operator,
        column_kappa * slope,
        precision=lax.Precision.HIGHEST,
        preferred_element_type=jnp.float32,
    )
    return column_field + axial_step * column_mask[None, :] * second


def to_columns(moved):
    return lax.all_to_all(moved, "hgt", split_axis=1, concat_axis=0, tiled=True)


def to_slabs(result):
    return lax.all_to_all(result, "hgt", split_axis=0, concat_axis=1, tiled=True)


def column_body(
    thermal_field,
    thermal_diffusivity,
    boundary_group_lookup,
    boundary_entry_conductances,
    exported_boundary_groups,
    domain_group_totals,
    pipe_cavity_indicator,
    boundary_vertex_matrix,
):
    layer_sample_number, plane_vertices = thermal_field.shape
    width = boundary_vertex_matrix.shape[0]
    group_size = max(1, 128 // width)
    spread = jnp.kron(jnp.eye(group_size, dtype=jnp.float32), boundary_vertex_matrix)
    block_ids = jnp.arange(plane_vertices) // width
    live_groups = block_ids < domain_group_totals[0]
    slab_mask = jnp.where(live_groups & (pipe_cavity_indicator == 0), 1.0, 0.0).astype(jnp.float32)
    spans = lax.axis_size("hgt")
    column_count = plane_vertices // spans
    column_start = lax.axis_index("hgt") * column_count
    column_mask = lax.dynamic_slice_in_dim(slab_mask, column_start, column_count, 0)
    operator = cheb_matrix(layer_sample_number * spans)
    present_solution = jnp.where(live_groups[None, :], thermal_field, jnp.float32(0.0))
    moved = conduct(
        present_solution,
        boundary_group_lookup,
        boundary_entry_conductances,
        exported_boundary_groups,
        spread,
        slab_mask,
        width,
    )
    column_field, kappa_fixed = (
        lax.all_to_all(moved, "hgt", split_axis=1, concat_axis=0, tiled=True),
        lax.all_to_all(thermal_diffusivity, "hgt", split_axis=1, concat_axis=0, tiled=True),
    )
    result = axial(column_field, kappa_fixed, operator, column_mask)
    present_solution = to_slabs(result)
    moved = conduct(
        present_solution,
        boundary_group_lookup,
        boundary_entry_conductances,
        exported_boundary_groups,
        spread,
        slab_mask,
        width,
    )
    result = axial(to_columns(moved), kappa_fixed, operator, column_mask)
    present_solution = to_slabs(result)
    return present_solution


def body(field, kappa, lookup, conductance, exported, totals, pipe, matrix):
    spans = lax.axis_size("hgt")
    factors = slab_factors(field.shape[0] * spans, spans)
    args = (field, kappa, lookup, conductance, exported, totals, pipe, matrix)
    if factors is None or 2 * matrix.shape[0] != lanes:
        return column_body(*args)
    return slab_body(factors, *args)


def solution(mesh):
    in_specs = (
        P("hgt", ("grp", "xs")),
        P("hgt", ("grp", "xs")),
        P("xs", None),
        P("xs", None),
        P("xs", None, None),
        P("xs"),
        P("xs"),
        P(),
    )
    out_specs = P("hgt", ("grp", "xs"))
    return jax.shard_map(body, mesh=mesh, in_specs=in_specs, out_specs=out_specs, check_vma=False)
```

```python
import functools
import math

import ml_dtypes
import numpy as np
import jax
import jax.numpy as jnp
from jax import lax
from jax.experimental import pallas as pl
from jax.experimental.pallas import tpu as pltpu
from jax.sharding import PartitionSpec as P

axial_step = 0.5
lanes = 128
near_rows = 12
far_rows = 4
joint_near_rows = 16
joint_far_rows = 8
carried_rows = 24


def cheb_exact(order):
    index = np.arange(order, dtype=np.float64)
    angle = math.pi / (2.0 * (order - 1))
    row, col = index[:, None], index[None, :]
    difference = -2.0 * np.sin((row + col) * angle) * np.sin((row - col) * angle)
    weight = np.ones(order)
    weight[0] = weight[-1] = 2.0
    parity = np.where((row + col) % 2 == 0, 1.0, -1.0)
    off_diag = row != col
    entries = np.where(
        off_diag, weight[:, None] / weight[None, :] * parity / np.where(off_diag, difference, 1.0), 0.0
    )
    entries = entries - np.diag(entries.sum(axis=1))
    sine = np.sin(np.minimum(index, order - 1 - index) * (2.0 * angle))
    return -sine[:, None] * entries / (order - 1)


def row_basis(block, rank):
    return np.linalg.svd(block, full_matrices=False)[2][:rank]


def halves(matrix):
    high = matrix.astype(ml_dtypes.bfloat16)
    return high, (matrix - high.astype(np.float64)).astype(ml_dtypes.bfloat16)


def pad_to(matrix, rows, cols):
    return np.pad(matrix, ((0, rows - matrix.shape[0]), (0, cols - matrix.shape[1])))


def round_up(size, step):
    return -(-size // step) * step


def as_left(matrix):
    high, low = halves(pad_to(matrix, matrix.shape[0], round_up(matrix.shape[1], 16)))
    return np.concatenate([high, high, low], axis=1)


def fold(rows, half, axis):
    whole = rows.shape[axis] // 8 * 8
    head, tail = np.split(rows, [whole], axis=axis)
    if not tail.shape[axis]:
        return head, tail
    zeros = np.zeros_like(tail)
    return head, np.concatenate([zeros, tail] if half else [tail, zeros], axis=axis)


def folded(parts, half, axis):
    pairs = [fold(part, half, axis) for part in parts]
    return np.concatenate([head for head, _ in pairs] + [tail for _, tail in pairs], axis=axis)


def turns(spans):
    return list(range(spans - 1, 0, -1))


@functools.lru_cache(maxsize=None)
def slab_factors(order, spans):
    slab = order // spans
    if spans & (spans - 1) or spans > 4 or slab < 128:
        return None
    full = cheb_exact(order)
    block = lambda s, t: full[s * slab : (s + 1) * slab, t * slab : (t + 1) * slab]
    near = {x: any(abs(s - (s ^ x)) == 1 for s in range(spans)) for x in turns(spans)}
    ranks = {x: near_rows if close else far_rows for x, close in near.items()}
    joint_ranks = {x: joint_near_rows if close else joint_far_rows for x, close in near.items()}
    first, joint = {}, {}
    carried, onward, left = {}, {}, {}
    for s in range(spans):
        others = [t for t in range(spans) if t != s]
        u, sigma, vt = np.linalg.svd(np.concatenate([block(s, t) for t in others], axis=1), full_matrices=False)
        left[s] = u[:, :carried_rows]
        rows = sigma[:carried_rows, None] * vt[:carried_rows]
        carried[s] = {t: rows[:, i * slab : (i + 1) * slab] for i, t in enumerate(others)}
        onward[s] = sum(carried[s][t] @ full[t * slab : (t + 1) * slab] for t in others)
        for t in others:
            first[s, t] = row_basis(block(s, t), ranks[s ^ t])
            joint[s, t] = row_basis(
                np.concatenate([block(s, t), onward[s][:, t * slab : (t + 1) * slab]], axis=0), joint_ranks[s ^ t]
            )
    sets = {}

    def add(name, matrix):
        sets.setdefault(name, []).append(as_left(matrix))

    for s in range(spans):
        partners = [s ^ x for x in turns(spans)]
        cut = lambda t: slice(t * slab, (t + 1) * slab)
        firsts = [np.concatenate([block(s, t), carried[s][t]], axis=0) @ first[s, t].T for t in partners]
        joints = [np.concatenate([block(s, t), onward[s][:, cut(t)]], axis=0) @ joint[s, t].T for t in partners]
        for half in range(2):
            add("send_half%d" % half, folded([first[t, s] for t in partners], half, 0))
            add("far_half%d" % half, folded(firsts, half, 1))
        add("send_rows", folded([first[t, s] for t in partners], 0, 0))
        add("send_joint", np.concatenate([joint[t, s] for t in partners], axis=0))
        add("far_joint", np.concatenate(joints, axis=1))
        add("local", np.concatenate([block(s, s), onward[s][:, cut(s)]], axis=0))
        add("onward", np.concatenate([block(s, s), left[s]], axis=1))
    return dict(
        ranks=list(ranks.values()), joint_ranks=list(joint_ranks.values()), sets={name: np.stack(parts) for name, parts in sets.items()}
    )


def split(values):
    high = values.astype(jnp.bfloat16)
    return high, (values - high.astype(jnp.float32)).astype(jnp.bfloat16)


def left_product(left, values):
    short = left.shape[1] // 3 - values.shape[0]
    if short:
        values = jnp.concatenate([values, jnp.zeros((short, values.shape[1]), jnp.float32)], axis=0)
    high, low = split(values)
    return jnp.dot(left, jnp.concatenate([high, low, high], axis=0), preferred_element_type=jnp.float32)


def right_product(values, right):
    high, low = split(values)
    return jnp.dot(jnp.concatenate([high, low, high], axis=1), right, preferred_element_type=jnp.float32)


def low_half():
    return lax.broadcasted_iota(jnp.int32, (1, lanes), 1) < lanes // 2


def tile_at(tile):
    return slice(tile * lanes, (tile + 1) * lanes)


def chunks(width):
    step = min(width, 512)
    return [slice(start, start + step) for start in range(0, width, step)]


def load(copies, sems):
    started = [pltpu.make_async_copy(source, target, sems.at[i]) for i, (source, target) in enumerate(copies)]
    for copy in started:
        copy.start()
    return started


def sides():
    first = lax.axis_index("xs") % 2
    return first, 1 - first


def take_face(source, exported, side):
    tiles = []
    for tile in range(exported.shape[1] // 2):
        parts = []
        for place in range(2):
            index = exported[side, 2 * tile + place]
            value = source[:, pl.ds(pl.multiple_of(index // 2 * lanes, lanes), lanes)]
            parts.append(jnp.where(index % 2 == place, value, pltpu.roll(value, lanes // 2, 1)))
        tiles.append(jnp.where(low_half(), parts[0], parts[1]))
    return jnp.concatenate(tiles, axis=1)


def faces_kernel(exported, field, first, second, faces, near, sems):
    got = load([(exported, faces), (field.at[:, pl.ds(0, near.shape[1])], near)], sems)
    for copy in got:
        copy.wait()
    for side, out in zip(sides(), (first, second)):
        out[...] = take_face(near, faces, side)


def prepare_kernel(count, total, pipe, matrix, field, *refs):
    stacks, (mask, spread, state, moments), outs = refs[:count], refs[count : count + 4], refs[count + 4 : 2 * count + 4]
    holes, block_matrix, values, sems = refs[2 * count + 4 :]
    where = lax.axis_index("hgt")
    pairs = [(matrix, block_matrix), (pipe, holes), (field, values)]
    got = load(pairs + [(stack.at[where], out) for stack, out in zip(stacks, outs)], sems)
    got[0].wait()
    width = matrix.shape[0]
    size = spread.shape[1]
    wide = jnp.concatenate([block_matrix[...]] * (size // width), axis=1)
    tall = jnp.concatenate([wide] * (size // width), axis=0)
    row = lax.broadcasted_iota(jnp.int32, tall.shape, 0) // width
    col = lax.broadcasted_iota(jnp.int32, tall.shape, 1) // width
    high, low = split(jnp.where(row == col, tall, 0.0))
    spread[...] = jnp.concatenate([high, high, low], axis=0)
    got[1].wait()
    block = lax.broadcasted_iota(jnp.int32, mask.shape, 1) // width
    live = block < total[0]
    mask[...] = jnp.where(live & (holes[...] == 0), 1.0, 0.0).astype(jnp.float32)
    for copy in got[2:]:
        copy.wait()
    for piece in chunks(field.shape[1]):
        state[:, piece] = jnp.where(live[:, piece], values[:, piece], 0.0)
        moments[:, piece] = left_product(outs[0][...], state[:, piece])


def fill(extended, tile, value):
    extended[0, tile] = value
    extended[1, tile] = pltpu.roll(value, lanes // 2, 1)


def fill_own(extended, own):
    tiles = own.shape[1] // lanes
    for tile in range(tiles):
        fill(extended, tile, own[:, tile_at(tile)])
    fill(extended, extended.shape[1] - 1, jnp.zeros(extended.shape[2:], jnp.float32))


def fill_rim(extended, first, second):
    rim = first.shape[1] // lanes
    start = extended.shape[1] - 1 - 2 * rim
    for side, values in zip(sides(), (first, second)):
        for tile in range(rim):
            fill(extended, start + side * rim + tile, values[:, tile_at(tile)])


def conducted(lookup, conductance, mask, spread, extended, gathered, pieces):
    half = low_half()
    per = spread.shape[1] // lanes
    for piece in pieces:
        start = piece.start // lanes
        for tile in range(start, piece.stop // lanes):
            low, high = 2 * tile, 2 * tile + 1
            total = jnp.where(half, conductance[0, low], conductance[0, high]) * extended[0, tile]
            for slot in range(1, lookup.shape[0]):
                one, two = lookup[slot, low], lookup[slot, high]
                value = jnp.where(half, extended[one % 2, one // 2], extended[1 - two % 2, two // 2])
                total = total + jnp.where(half, conductance[slot, low], conductance[slot, high]) * value
            gathered[:, tile_at(tile)] = total
        moved = []
        for tile in range(start, piece.stop // lanes, per):
            part = slice(tile * lanes, (tile + per) * lanes)
            own = jnp.concatenate([extended[0, tile + i] for i in range(per)], axis=1)
            moved.append(own + mask[:, part] * right_product(gathered[:, part], spread[...]))
        yield piece, jnp.concatenate(moved, axis=1)


def store_rows(moved, outs, piece):
    start = 0
    for out in outs:
        out[:, piece] = moved[start : start + out.shape[0]]
        start += out.shape[0]


def stacked(refs, piece):
    return jnp.concatenate([ref[:, piece] for ref in refs], axis=0)


def folded_views(refs, piece, nodes):
    half = piece.start // (nodes // 2)
    heads = [(ref, piece) for ref in refs if ref.shape[1] >= nodes]
    tails = []
    for ref in refs:
        start = (nodes if ref.shape[1] >= nodes else 0) + piece.start - half * (nodes // 2)
        if ref.shape[1] != nodes:
            tails.append((ref, slice(start, start + piece.stop - piece.start)))
    return half, heads, tails


def store_folded(moved, refs, piece, nodes):
    half, heads, tails = folded_views(refs, piece, nodes)
    for i, (ref, part) in enumerate(heads + tails):
        value = moved[8 * i : 8 * i + 8]
        ref[:, part] = ref[:, part] + value if half and i >= len(heads) else value


def load_folded(refs, piece, nodes):
    half, heads, tails = folded_views(refs, piece, nodes)
    return half, jnp.concatenate([ref[:, part] for ref, part in heads + tails], axis=0)


def moments_kernel(lookup, conductance, moments, first, second, mask, spread, send, *refs):
    outs, (table, weight, extended, gathered, sems) = refs[:-5], refs[-5:]
    nodes = moments.shape[1]
    got = load([(lookup, table), (conductance, weight)], sems)
    fill_own(extended, moments)
    fill_rim(extended, left_product(send[...], first[...]), left_product(send[...], second[...]))
    for copy in got:
        copy.wait()
    whole = 8 * sum(out.shape[1] >= nodes for out in outs)
    for piece, values in conducted(table, weight, mask, spread, extended, gathered, chunks(nodes)):
        if piece.start >= nodes // 2:
            tails = [pltpu.roll(values[i : i + 8], 4, 0) for i in range(whole, values.shape[0], 8)]
            values = jnp.concatenate([values[:whole]] + tails, axis=0)
        store_folded(values, outs, piece, nodes)


def first_kernel(lookup, conductance, field, first, second, mask, spread, local, out, slope, *scratch):
    table, weight, extended, gathered, sems = scratch
    slab = field.shape[0]
    got = load([(lookup, table), (conductance, weight)], sems)
    fill_own(extended, field)
    fill_rim(extended, first, second)
    for copy in got:
        copy.wait()
    for piece, values in conducted(table, weight, mask, spread, extended, gathered, chunks(field.shape[1])):
        out[:, piece] = values
        slope[:, piece] = left_product(local[:slab], values)


def flux_kernel(spans, slope, *refs):
    got, (kappa, send), fars, (flux, carried), outs = (
        refs[: spans - 1],
        refs[spans - 1 : spans + 1],
        refs[spans + 1 : spans + 3],
        refs[spans + 3 : spans + 5],
        refs[spans + 5 :],
    )
    slab, nodes = slope.shape
    for piece in chunks(nodes):
        half, rows = load_folded(got, piece, nodes)
        far = left_product(fars[half][...], rows)
        carried[:, piece] = far[slab:]
        value = kappa[:, piece] * (slope[:, piece] + far[:slab])
        flux[:, piece] = value
        store_rows(left_product(send[...], value), outs, piece)


def rim_matrix(table, weight, mask, block_matrix, own_blocks, high, low):
    width = block_matrix.shape[0]
    slots, blocks = table.shape
    for piece in chunks(mask.shape[1]):
        block = (piece.start + lax.broadcasted_iota(jnp.int32, (blocks, piece.stop - piece.start), 1)) // width
        pick = jnp.where(block == lax.broadcasted_iota(jnp.int32, block.shape, 0), 1.0, 0.0)
        spread_out = lambda rows: jnp.dot(
            rows, pick, precision=lax.Precision.HIGHEST, preferred_element_type=jnp.float32
        )
        index = spread_out(table[...].astype(jnp.float32))
        value = spread_out(weight[...]) * mask[:, piece]
        wide = jnp.concatenate([block_matrix[...]] * (block.shape[1] // width), axis=1)
        for received in range(high.shape[0] // width):
            hit = jnp.where(jnp.abs(index - (own_blocks + received)) < 0.5, value, 0.0)
            gain = jnp.sum(hit[1:slots], axis=0, keepdims=True)
            rows = slice(received * width, (received + 1) * width)
            high[rows, piece], low[rows, piece] = split(wide * gain)


def local_kernel(lookup, conductance, matrix, field, carried, flux, mask, local, out, high, low, *scratch):
    table, weight, block_matrix, sems = scratch
    slab = field.shape[0]
    got = load([(lookup, table), (conductance, weight), (matrix, block_matrix)], sems)
    for piece in chunks(field.shape[1]):
        step = axial_step * mask[:, piece] * left_product(local[...], flux[:, piece])
        out[:slab, piece] = field[:, piece] + step[:slab]
        out[slab:, piece] = carried[:, piece] + step[slab:]
    for copy in got:
        copy.wait()
    rim_matrix(table, weight, mask, block_matrix, field.shape[1] // block_matrix.shape[0], high, low)


def rim_kernel(spans, exported, base, mask, far, *refs):
    got, (first, second, faces, sems) = refs[: spans - 1], refs[spans - 1 :]
    (copy,) = load([(exported, faces)], sems)
    copy.wait()
    for side, out in zip(sides(), (first, second)):
        rows = jnp.concatenate([take_face(ref, faces, side) for ref in got], axis=0)
        out[...] = take_face(base, faces, side) + axial_step * take_face(mask, faces, side) * left_product(far[...], rows)


def close_kernel(spans, lookup, conductance, base, mask, spread, far, onward, *refs):
    got, (out, slope, table, weight, extended, gathered, sems) = refs[: spans - 1], refs[spans - 1 :]
    slab, nodes = out.shape
    copies = load([(lookup, table), (conductance, weight)], sems)
    for piece in chunks(nodes):
        values = base[:, piece] + axial_step * mask[:, piece] * left_product(far[...], stacked(got, piece))
        out[:, piece] = values[:slab]
        own = left_product(onward[...], values)
        for tile in range(piece.start // lanes, piece.stop // lanes):
            fill(extended, tile, own[:, tile * lanes - piece.start : (tile + 1) * lanes - piece.start])
    for tile in range(nodes // lanes, extended.shape[1]):
        extended[0, tile] = jnp.zeros(extended.shape[2:], jnp.float32)
        extended[1, tile] = jnp.zeros(extended.shape[2:], jnp.float32)
    for copy in copies:
        copy.wait()
    for piece, values in conducted(table, weight, mask, spread, extended, gathered, chunks(nodes)):
        slope[:, piece] = values


def second_kernel(slope, first, second, high, low, kappa, onward, *refs):
    sends, flux, outs = refs[:2], refs[2], refs[3:]
    slab, nodes = slope.shape
    rim = first.shape[1]
    received = []
    for side, values in zip(sides(), (first, second)):
        top, bottom = split(left_product(onward[...], values[...]))
        received.append((pl.ds(pl.multiple_of(side * rim, rim), rim), top, jnp.concatenate([top, bottom], axis=0)))
    for piece in chunks(nodes):
        total = slope[:, piece]
        for rows, top, both in received:
            main = jnp.dot(both, high[rows, piece], preferred_element_type=jnp.float32)
            total = total + (main[:slab] + main[slab:])
            total = total + jnp.dot(top, low[rows, piece], preferred_element_type=jnp.float32)
        value = kappa[:, piece] * total
        flux[:, piece] = value
        half = piece.start // (nodes // 2)
        store_folded(left_product(sends[half][...], value), outs, piece, nodes)


def rest_kernel(lookup, conductance, field, flux, first, second, mask, spread, local, out, *scratch):
    table, weight, extended, gathered, sems = scratch
    slab = field.shape[0]
    got = load([(lookup, table), (conductance, weight)], sems)
    fill_own(extended, field)
    fill_rim(extended, first[:slab], second[:slab])
    for copy in got:
        copy.wait()
    for piece, values in conducted(table, weight, mask, spread, extended, gathered, chunks(field.shape[1])):
        out[:, piece] = values + axial_step * mask[:, piece] * left_product(local[:slab], flux[:, piece])


def last_kernel(spans, base, mask, *refs):
    fars, got, (out, values, sems) = refs[:2], refs[2 : spans + 1], refs[spans + 1 :]
    slab, nodes = base.shape
    copies = []
    for i, piece in enumerate(chunks(nodes)):
        half, rows = load_folded(got, piece, nodes)
        values[:, piece] = base[:, piece] + axial_step * mask[:, piece] * left_product(fars[half][:slab], rows)
        part = pl.ds(piece.start, piece.stop - piece.start)
        copies.append(pltpu.make_async_copy(values.at[:, part], out.at[:, part], sems.at[i]))
        copies[-1].start()
    for copy in copies:
        copy.wait()


def in_place(array):
    return pltpu.with_memory_space_constraint(array, pltpu.HBM)


def call(kernel, far, near, outs, scratch=(), flops=0, name=None, scalars=(), out_space=pltpu.VMEM):
    outs = [out if isinstance(out, jax.ShapeDtypeStruct) else jax.ShapeDtypeStruct(out, jnp.float32) for out in outs]
    size = sum(4 * array.size for array in [*near, *outs])
    spaces = [(scalars, pltpu.SMEM), (far, pltpu.HBM), (near, pltpu.VMEM)]
    return pl.pallas_call(
        kernel,
        in_specs=[pl.BlockSpec(memory_space=space) for arrays, space in spaces for _ in arrays],
        out_specs=[pl.BlockSpec(memory_space=out_space)] * len(outs),
        out_shape=outs,
        scratch_shapes=list(scratch),
        compiler_params=pltpu.CompilerParams(vmem_limit_bytes=24 * 2**20),
        cost_estimate=pl.CostEstimate(flops=flops, bytes_accessed=size, transcendentals=0),
        name=name,
    )(*scalars, *[in_place(array) for array in far], *near)


def trade_faces(first, second):
    count = lax.axis_size("xs")
    swap = lambda start: [pair for i in range(start, count - 1, 2) for pair in ((i, i + 1), (i + 1, i))]
    return lax.ppermute(first, "xs", swap(1)), lax.ppermute(second, "xs", swap(0))


def trade_slabs(parts):
    count = lax.axis_size("hgt")
    return [lax.ppermute(part, "hgt", [(i, i ^ x) for i in range(count)]) for x, part in zip(turns(count), parts)]


def slab_body(factors, field, kappa, lookup, conductance, exported, totals, pipe, matrix):
    slab, nodes = field.shape
    spans = lax.axis_size("hgt")
    faces = exported.shape[1:]
    rim = faces[1] * matrix.shape[0]
    tables = [lookup.T, conductance.T]
    exported = exported.reshape(faces)
    tall = slab + carried_rows
    tiles = (nodes + 2 * rim) // lanes + 1
    sent = [(8, rank // 8 * nodes + (rank % 8 > 0) * nodes // 2) for rank in factors["ranks"]]
    sent_joint = [(rank, nodes) for rank in factors["joint_ranks"]]
    whole = (slab, nodes)
    work = 2 * nodes * slab * slab

    def conduct_scratch(height):
        return [
            pltpu.SMEM(tables[0].shape, jnp.int32),
            pltpu.SMEM(tables[1].shape, jnp.float32),
            pltpu.VMEM((2, tiles, height, lanes), jnp.float32),
            pltpu.VMEM((height, nodes), jnp.float32),
            pltpu.SemaphoreType.DMA((2,)),
        ]

    face_scratch = pltpu.SMEM(faces, jnp.int32)
    first, second = call(
        faces_kernel,
        [exported, field],
        [],
        [(slab, rim)] * 2,
        [face_scratch, pltpu.VMEM((slab, nodes // 2), jnp.float32), pltpu.SemaphoreType.DMA((2,))],
        name="faces",
    )
    left, right = trade_faces(first, second)
    names = ["send_rows"] + sorted(name for name in factors["sets"] if name != "send_rows")
    stacks = [jnp.asarray(factors["sets"][name]) for name in names]
    height = stacks[0].shape[1]
    spread = jax.ShapeDtypeStruct((6 * lanes, 2 * lanes), jnp.bfloat16)
    mask, spread, state, moments, *own = call(
        functools.partial(prepare_kernel, len(stacks)),
        [pipe.reshape(1, nodes), matrix, field, *stacks],
        [],
        [(1, nodes), spread, whole, (height, nodes)]
        + [jax.ShapeDtypeStruct(stack.shape[1:], jnp.bfloat16) for stack in stacks],
        [
            pltpu.VMEM((1, nodes), jnp.int32),
            pltpu.VMEM(matrix.shape, jnp.float32),
            pltpu.VMEM(whole, jnp.float32),
            pltpu.SemaphoreType.DMA((3 + len(stacks),)),
        ],
        work,
        "prepare",
        [totals],
    )
    own = dict(zip(names, own))
    sends = [own["send_half0"], own["send_half1"]]
    fars = [own["far_half0"], own["far_half1"]]
    parts = call(
        moments_kernel, tables, [moments, left, right, mask, spread, own["send_rows"]], sent, conduct_scratch(height), name="moments"
    )
    parts = trade_slabs(parts)
    state, slope = call(
        first_kernel,
        tables,
        [state, left, right, mask, spread, own["local"]],
        [whole, whole],
        conduct_scratch(slab),
        2 * work,
        "first",
    )
    flux, carried, *joint = call(
        functools.partial(flux_kernel, spans),
        [],
        [slope, *parts, kappa, own["send_joint"], *fars],
        [whole, (carried_rows, nodes)] + sent_joint,
        name="flux",
    )
    joint = trade_slabs(joint)
    half_matrix = jax.ShapeDtypeStruct((2 * rim, nodes), jnp.bfloat16)
    base, high, low = call(
        local_kernel,
        [*tables, matrix],
        [state, carried, flux, mask, own["local"]],
        [(tall, nodes), half_matrix, half_matrix],
        [
            pltpu.VMEM(tables[0].shape, jnp.int32),
            pltpu.VMEM(tables[1].shape, jnp.float32),
            pltpu.VMEM(matrix.shape, jnp.float32),
            pltpu.SemaphoreType.DMA((3,)),
        ],
        2 * work,
        "local",
    )
    first, second = call(
        functools.partial(rim_kernel, spans),
        [exported],
        [base, mask, own["far_joint"], *joint],
        [(tall, rim)] * 2,
        [face_scratch, pltpu.SemaphoreType.DMA((1,))],
        name="rim",
    )
    left, right = trade_faces(first, second)
    state, slope = call(
        functools.partial(close_kernel, spans),
        tables,
        [base, mask, spread, own["far_joint"], own["onward"], *joint],
        [whole, whole],
        conduct_scratch(slab),
        2 * work,
        "close",
    )
    flux, *parts = call(
        second_kernel,
        [],
        [slope, left, right, high, low, kappa, own["onward"], *sends],
        [whole] + sent,
        name="second",
    )
    parts = trade_slabs(parts)
    (base,) = call(
        rest_kernel,
        tables,
        [state, flux, left, right, mask, spread, own["local"]],
        [whole],
        conduct_scratch(slab),
        2 * work,
        "rest",
    )
    (state,) = call(
        functools.partial(last_kernel, spans),
        [],
        [base, mask, *fars, *parts],
        [whole],
        [pltpu.VMEM(whole, jnp.float32), pltpu.SemaphoreType.DMA((len(chunks(nodes)),))],
        name="last",
        out_space=pltpu.HBM,
    )
    return state


def padded_2(cells, sides, width):
    for axis, dim in sides:
        count = lax.axis_size(axis)
        ends = count - 1
        head = lax.slice_in_dim(cells, 0, width, axis=dim)
        tail = lax.slice_in_dim(cells, cells.shape[dim] - width, cells.shape[dim], axis=dim)
        cells = jnp.concatenate(
            [
                lax.ppermute(tail, axis, [(i, (i + 1) % count) for i in range(ends)]),
                cells,
                lax.ppermute(head, axis, [((i + 1) % count, i) for i in range(ends)]),
            ],
            axis=dim,
        )
    return cells


def cheb_matrix(order):
    index = jnp.arange(order)
    row_f = index[:, None].astype(jnp.float32)
    col_f = index[None, :].astype(jnp.float32)
    angle = math.pi / (2.0 * (order - 1))
    difference = -2.0 * jnp.sin((row_f + col_f) * angle) * jnp.sin((row_f - col_f) * angle)
    ends = (index == 0) | (index == order - 1)
    weight = jnp.where(ends, 2.0, 1.0).astype(jnp.float32)
    parity = jnp.where((index[:, None] + index[None, :]) % 2 == 0, 1.0, -1.0).astype(jnp.float32)
    off_diag = index[:, None] != index[None, :]
    safe_diff = jnp.where(off_diag, difference, jnp.float32(1.0))
    entries = jnp.where(
        off_diag, weight[:, None] / weight[None, :] * parity / safe_diff, jnp.float32(0.0)
    )
    entries = entries - jnp.diag(jnp.sum(entries, axis=1))
    mirror = jnp.minimum(index, order - 1 - index).astype(jnp.float32)
    sine = jnp.sin(mirror * (2.0 * angle))
    return -sine[:, None] * entries / (order - 1)


def slot_sum(source, indices, boundary_entry_conductances, total):
    for slot_index in range(indices.shape[1]):
        picked = source[:, indices[:, slot_index], :]
        total = total + boundary_entry_conductances[None, :, slot_index, None] * picked
    return total


def conduct(
    present_solution,
    boundary_group_lookup,
    boundary_entry_conductances,
    exported_boundary_groups,
    spread,
    slab_mask,
    width,
):
    height, plane_vertices = present_solution.shape
    blocks = plane_vertices // width
    face_count = exported_boundary_groups.shape[2]
    blocked = present_solution.reshape(height, blocks, width)
    outgoing = jnp.concatenate(
        [
            blocked[:, exported_boundary_groups[0, 0], :],
            blocked[:, exported_boundary_groups[0, 1], :],
        ],
        axis=1,
    )
    outgoing = outgoing.reshape(height, 2 * face_count * width)
    rim_width = face_count * width
    padded = padded_2(outgoing, (("xs", 1),), rim_width)
    from_left = padded[:, :rim_width].reshape(height, face_count, width)
    from_right = padded[:, padded.shape[1] - rim_width :].reshape(height, face_count, width)
    empty = jnp.zeros((height, 1, width), jnp.float32)
    gathered = jnp.zeros((height, blocks, width), jnp.float32)
    extended = jnp.concatenate([blocked, from_left, from_right, empty], axis=1)
    gathered = slot_sum(extended, boundary_group_lookup, boundary_entry_conductances, gathered)
    coupled = jnp.dot(
        gathered.reshape(-1, spread.shape[0]),
        spread,
        precision=lax.Precision.HIGHEST,
        preferred_element_type=jnp.float32,
    ).reshape(height, plane_vertices)
    return present_solution + slab_mask[None, :] * coupled


def axial(column_field, column_kappa, operator, column_mask):
    slope = jnp.dot(
        operator, column_field, precision=lax.Precision.HIGHEST, preferred_element_type=jnp.float32
    )
    second = jnp.dot(
        operator,
        column_kappa * slope,
        precision=lax.Precision.HIGHEST,
        preferred_element_type=jnp.float32,
    )
    return column_field + axial_step * column_mask[None, :] * second


def to_columns(moved):
    return lax.all_to_all(moved, "hgt", split_axis=1, concat_axis=0, tiled=True)


def to_slabs(result):
    return lax.all_to_all(result, "hgt", split_axis=0, concat_axis=1, tiled=True)


def column_body(
    thermal_field,
    thermal_diffusivity,
    boundary_group_lookup,
    boundary_entry_conductances,
    exported_boundary_groups,
    domain_group_totals,
    pipe_cavity_indicator,
    boundary_vertex_matrix,
):
    layer_sample_number, plane_vertices = thermal_field.shape
    width = boundary_vertex_matrix.shape[0]
    group_size = max(1, 128 // width)
    spread = jnp.kron(jnp.eye(group_size, dtype=jnp.float32), boundary_vertex_matrix)
    block_ids = jnp.arange(plane_vertices) // width
    live_groups = block_ids < domain_group_totals[0]
    slab_mask = jnp.where(live_groups & (pipe_cavity_indicator == 0), 1.0, 0.0).astype(jnp.float32)
    spans = lax.axis_size("hgt")
    column_count = plane_vertices // spans
    column_start = lax.axis_index("hgt") * column_count
    column_mask = lax.dynamic_slice_in_dim(slab_mask, column_start, column_count, 0)
    operator = cheb_matrix(layer_sample_number * spans)
    present_solution = jnp.where(live_groups[None, :], thermal_field, jnp.float32(0.0))
    moved = conduct(
        present_solution,
        boundary_group_lookup,
        boundary_entry_conductances,
        exported_boundary_groups,
        spread,
        slab_mask,
        width,
    )
    column_field, kappa_fixed = (
        lax.all_to_all(moved, "hgt", split_axis=1, concat_axis=0, tiled=True),
        lax.all_to_all(thermal_diffusivity, "hgt", split_axis=1, concat_axis=0, tiled=True),
    )
    result = axial(column_field, kappa_fixed, operator, column_mask)
    present_solution = to_slabs(result)
    moved = conduct(
        present_solution,
        boundary_group_lookup,
        boundary_entry_conductances,
        exported_boundary_groups,
        spread,
        slab_mask,
        width,
    )
    result = axial(to_columns(moved), kappa_fixed, operator, column_mask)
    present_solution = to_slabs(result)
    return present_solution


def body(field, kappa, lookup, conductance, exported, totals, pipe, matrix):
    spans = lax.axis_size("hgt")
    factors = slab_factors(field.shape[0] * spans, spans)
    args = (field, kappa, lookup, conductance, exported, totals, pipe, matrix)
    if factors is None or 2 * matrix.shape[0] != lanes:
        return column_body(*args)
    return slab_body(factors, *args)


def solution(mesh):
    in_specs = (
        P("hgt", ("grp", "xs")),
        P("hgt", ("grp", "xs")),
        P("xs", None),
        P("xs", None),
        P("xs", None, None),
        P("xs"),
        P("xs"),
        P(),
    )
    out_specs = P("hgt", ("grp", "xs"))
    return jax.shard_map(body, mesh=mesh, in_specs=in_specs, out_specs=out_specs, check_vma=False)
```

```python
import functools
import math

import ml_dtypes
import numpy as np
import jax
import jax.numpy as jnp
from jax import lax
from jax.experimental import pallas as pl
from jax.experimental.pallas import tpu as pltpu
from jax.sharding import PartitionSpec as P

axial_step = 0.5
lanes = 128
near_rows = 12
far_rows = 4
joint_near_rows = 16
joint_far_rows = 8
carried_rows = 24


def cheb_exact(order):
    index = np.arange(order, dtype=np.float64)
    angle = math.pi / (2.0 * (order - 1))
    row, col = index[:, None], index[None, :]
    difference = -2.0 * np.sin((row + col) * angle) * np.sin((row - col) * angle)
    weight = np.ones(order)
    weight[0] = weight[-1] = 2.0
    parity = np.where((row + col) % 2 == 0, 1.0, -1.0)
    off_diag = row != col
    entries = np.where(
        off_diag, weight[:, None] / weight[None, :] * parity / np.where(off_diag, difference, 1.0), 0.0
    )
    entries = entries - np.diag(entries.sum(axis=1))
    sine = np.sin(np.minimum(index, order - 1 - index) * (2.0 * angle))
    return -sine[:, None] * entries / (order - 1)


def row_basis(block, rank):
    return np.linalg.svd(block, full_matrices=False)[2][:rank]


def halves(matrix):
    high = matrix.astype(ml_dtypes.bfloat16)
    return high, (matrix - high.astype(np.float64)).astype(ml_dtypes.bfloat16)


def pad_to(matrix, rows, cols):
    return np.pad(matrix, ((0, rows - matrix.shape[0]), (0, cols - matrix.shape[1])))


def round_up(size, step):
    return -(-size // step) * step


def as_left(matrix):
    high, low = halves(pad_to(matrix, matrix.shape[0], round_up(matrix.shape[1], 16)))
    return np.concatenate([high, high, low], axis=1)


def fold(rows, half, axis):
    whole = rows.shape[axis] // 8 * 8
    head, tail = np.split(rows, [whole], axis=axis)
    if not tail.shape[axis]:
        return head, tail
    zeros = np.zeros_like(tail)
    return head, np.concatenate([zeros, tail] if half else [tail, zeros], axis=axis)


def folded(parts, half, axis):
    pairs = [fold(part, half, axis) for part in parts]
    return np.concatenate([head for head, _ in pairs] + [tail for _, tail in pairs], axis=axis)


def turns(spans):
    return list(range(spans - 1, 0, -1))


@functools.lru_cache(maxsize=None)
def slab_factors(order, spans):
    slab = order // spans
    if spans & (spans - 1) or spans > 4 or slab < 128:
        return None
    full = cheb_exact(order)
    block = lambda s, t: full[s * slab : (s + 1) * slab, t * slab : (t + 1) * slab]
    near = {x: any(abs(s - (s ^ x)) == 1 for s in range(spans)) for x in turns(spans)}
    ranks = {x: near_rows if close else far_rows for x, close in near.items()}
    joint_ranks = {x: joint_near_rows if close else joint_far_rows for x, close in near.items()}
    first, joint = {}, {}
    carried, onward, left = {}, {}, {}
    for s in range(spans):
        others = [t for t in range(spans) if t != s]
        u, sigma, vt = np.linalg.svd(np.concatenate([block(s, t) for t in others], axis=1), full_matrices=False)
        left[s] = u[:, :carried_rows]
        rows = sigma[:carried_rows, None] * vt[:carried_rows]
        carried[s] = {t: rows[:, i * slab : (i + 1) * slab] for i, t in enumerate(others)}
        onward[s] = sum(carried[s][t] @ full[t * slab : (t + 1) * slab] for t in others)
        for t in others:
            first[s, t] = row_basis(block(s, t), ranks[s ^ t])
            joint[s, t] = row_basis(
                np.concatenate([block(s, t), onward[s][:, t * slab : (t + 1) * slab]], axis=0), joint_ranks[s ^ t]
            )
    sets = {}

    def add(name, matrix):
        sets.setdefault(name, []).append(as_left(matrix))

    for s in range(spans):
        partners = [s ^ x for x in turns(spans)]
        cut = lambda t: slice(t * slab, (t + 1) * slab)
        firsts = [np.concatenate([block(s, t), carried[s][t]], axis=0) @ first[s, t].T for t in partners]
        joints = [np.concatenate([block(s, t), onward[s][:, cut(t)]], axis=0) @ joint[s, t].T for t in partners]
        for half in range(2):
            add("send_half%d" % half, folded([first[t, s] for t in partners], half, 0))
            add("far_half%d" % half, folded(firsts, half, 1))
        add("send_rows", folded([first[t, s] for t in partners], 0, 0))
        add("send_joint", np.concatenate([joint[t, s] for t in partners], axis=0))
        joint_far = np.concatenate(joints, axis=1)
        add("far_joint", joint_far)
        add("onward_far", axial_step * np.concatenate([block(s, s), left[s]], axis=1) @ joint_far)
        add("local", np.concatenate([block(s, s), onward[s][:, cut(s)]], axis=0))
        add("onward", np.concatenate([block(s, s), left[s]], axis=1))
    return dict(
        ranks=list(ranks.values()), joint_ranks=list(joint_ranks.values()), sets={name: np.stack(parts) for name, parts in sets.items()}
    )


def split(values):
    high = values.astype(jnp.bfloat16)
    return high, (values - high.astype(jnp.float32)).astype(jnp.bfloat16)


def left_product(left, values):
    short = left.shape[1] // 3 - values.shape[0]
    if short:
        values = jnp.concatenate([values, jnp.zeros((short, values.shape[1]), jnp.float32)], axis=0)
    high, low = split(values)
    return jnp.dot(left, jnp.concatenate([high, low, high], axis=0), preferred_element_type=jnp.float32)


def right_product(values, right):
    high, low = split(values)
    return jnp.dot(jnp.concatenate([high, low, high], axis=1), right, preferred_element_type=jnp.float32)


def low_half():
    return lax.broadcasted_iota(jnp.int32, (1, lanes), 1) < lanes // 2


def tile_at(tile):
    return slice(tile * lanes, (tile + 1) * lanes)


def chunks(width):
    step = min(width, 512)
    return [slice(start, start + step) for start in range(0, width, step)]


def load(copies, sems):
    started = [pltpu.make_async_copy(source, target, sems.at[i]) for i, (source, target) in enumerate(copies)]
    for copy in started:
        copy.start()
    return started


def sides():
    first = lax.axis_index("xs") % 2
    return first, 1 - first


def take_face(source, exported, side):
    tiles = []
    for tile in range(exported.shape[1] // 2):
        parts = []
        for place in range(2):
            index = exported[side, 2 * tile + place]
            value = source[:, pl.ds(pl.multiple_of((index >> 1) * lanes, lanes), lanes)]
            parts.append(jnp.where(index & 1 == place, value, pltpu.roll(value, lanes // 2, 1)))
        tiles.append(jnp.where(low_half(), parts[0], parts[1]))
    return jnp.concatenate(tiles, axis=1)


def faces_kernel(exported, field, first, second, faces, near, sems):
    got = load([(exported, faces), (field.at[:, pl.ds(0, near.shape[1])], near)], sems)
    for copy in got:
        copy.wait()
    for side, out in zip(sides(), (first, second)):
        out[...] = take_face(near, faces, side)


def prepare_kernel(count, total, pipe, matrix, field, *refs):
    stacks, (mask, spread, state, moments), outs = refs[:count], refs[count : count + 4], refs[count + 4 : 2 * count + 4]
    holes, block_matrix, values, sems = refs[2 * count + 4 :]
    where = lax.axis_index("hgt")
    pairs = [(matrix, block_matrix), (pipe, holes), (field, values)]
    got = load(pairs + [(stack.at[where], out) for stack, out in zip(stacks, outs)], sems)
    got[0].wait()
    width = matrix.shape[0]
    size = spread.shape[1]
    wide = jnp.concatenate([block_matrix[...]] * (size // width), axis=1)
    tall = jnp.concatenate([wide] * (size // width), axis=0)
    row = lax.broadcasted_iota(jnp.int32, tall.shape, 0) // width
    col = lax.broadcasted_iota(jnp.int32, tall.shape, 1) // width
    high, low = split(jnp.where(row == col, tall, 0.0))
    spread[...] = jnp.concatenate([high, high, low], axis=0)
    got[1].wait()
    block = lax.broadcasted_iota(jnp.int32, mask.shape, 1) // width
    live = block < total[0]
    mask[...] = jnp.where(live & (holes[...] == 0), 1.0, 0.0).astype(jnp.float32)
    for copy in got[2:]:
        copy.wait()
    for piece in chunks(field.shape[1]):
        state[:, piece] = jnp.where(live[:, piece], values[:, piece], 0.0)
        moments[:, piece] = left_product(outs[0][...], state[:, piece])


def fill(extended, tile, value):
    extended[2 * tile] = value
    extended[2 * tile + 1] = pltpu.roll(value, lanes // 2, 1)


def fill_own(extended, own):
    for tile in range(own.shape[1] // lanes):
        fill(extended, tile, own[:, tile_at(tile)])


def clear_from(extended, start):
    for entry in range(start, extended.shape[0]):
        extended[entry] = jnp.zeros(extended.shape[1:], jnp.float32)


def fill_rim(extended, first, second):
    rim = first.shape[1] // lanes
    start = extended.shape[0] // 2 - 1 - 2 * rim
    for side, values in zip(sides(), (first, second)):
        for tile in range(rim):
            fill(extended, start + side * rim + tile, values[:, tile_at(tile)])
    clear_from(extended, extended.shape[0] - 2)


def conducted(lookup, conductance, mask, spread, extended, gathered, pieces):
    half = low_half()
    per = spread.shape[1] // lanes
    for piece in pieces:
        start = piece.start // lanes
        for tile in range(start, piece.stop // lanes):
            low, high = 2 * tile, 2 * tile + 1
            total = jnp.where(half, conductance[0, low], conductance[0, high]) * extended[2 * tile]
            for slot in range(1, lookup.shape[0]):
                one, two = lookup[slot, low], lookup[slot, high]
                value = jnp.where(half, extended[one], extended[two ^ 1])
                total = total + jnp.where(half, conductance[slot, low], conductance[slot, high]) * value
            gathered[:, tile_at(tile)] = total
        moved = []
        for tile in range(start, piece.stop // lanes, per):
            part = slice(tile * lanes, (tile + per) * lanes)
            own = jnp.concatenate([extended[2 * (tile + i)] for i in range(per)], axis=1)
            moved.append(own + mask[:, part] * right_product(gathered[:, part], spread[...]))
        yield piece, jnp.concatenate(moved, axis=1)


def store_rows(moved, outs, piece):
    start = 0
    for out in outs:
        out[:, piece] = moved[start : start + out.shape[0]]
        start += out.shape[0]


def stacked(refs, piece):
    return jnp.concatenate([ref[:, piece] for ref in refs], axis=0)


def folded_views(refs, piece, nodes):
    half = piece.start // (nodes // 2)
    heads = [(ref, piece) for ref in refs if ref.shape[1] >= nodes]
    tails = []
    for ref in refs:
        start = (nodes if ref.shape[1] >= nodes else 0) + piece.start - half * (nodes // 2)
        if ref.shape[1] != nodes:
            tails.append((ref, slice(start, start + piece.stop - piece.start)))
    return half, heads, tails


def store_folded(moved, refs, piece, nodes):
    half, heads, tails = folded_views(refs, piece, nodes)
    for i, (ref, part) in enumerate(heads + tails):
        value = moved[8 * i : 8 * i + 8]
        ref[:, part] = ref[:, part] + value if half and i >= len(heads) else value


def load_folded(refs, piece, nodes):
    half, heads, tails = folded_views(refs, piece, nodes)
    return half, jnp.concatenate([ref[:, part] for ref, part in heads + tails], axis=0)


def moments_kernel(lookup, conductance, moments, first, second, mask, spread, send, *refs):
    outs, (table, weight, extended, gathered, sems) = refs[:-5], refs[-5:]
    nodes = moments.shape[1]
    got = load([(lookup, table), (conductance, weight)], sems)
    fill_own(extended, moments)
    fill_rim(extended, left_product(send[...], first[...]), left_product(send[...], second[...]))
    for copy in got:
        copy.wait()
    whole = 8 * sum(out.shape[1] >= nodes for out in outs)
    for piece, values in conducted(table, weight, mask, spread, extended, gathered, chunks(nodes)):
        if piece.start >= nodes // 2:
            tails = [pltpu.roll(values[i : i + 8], 4, 0) for i in range(whole, values.shape[0], 8)]
            values = jnp.concatenate([values[:whole]] + tails, axis=0)
        store_folded(values, outs, piece, nodes)


def first_kernel(lookup, conductance, field, first, second, mask, spread, local, out, slope, *scratch):
    table, weight, extended, gathered, sems = scratch
    slab = field.shape[0]
    got = load([(lookup, table), (conductance, weight)], sems)
    fill_own(extended, field)
    fill_rim(extended, first, second)
    for copy in got:
        copy.wait()
    for piece, values in conducted(table, weight, mask, spread, extended, gathered, chunks(field.shape[1])):
        out[:, piece] = values
        slope[:, piece] = left_product(local[:slab], values)


def flux_kernel(spans, slope, *refs):
    got, (kappa, send), fars, (flux, carried), outs = (
        refs[: spans - 1],
        refs[spans - 1 : spans + 1],
        refs[spans + 1 : spans + 3],
        refs[spans + 3 : spans + 5],
        refs[spans + 5 :],
    )
    slab, nodes = slope.shape
    for piece in chunks(nodes):
        half, rows = load_folded(got, piece, nodes)
        far = left_product(fars[half][...], rows)
        carried[:, piece] = far[slab:]
        value = kappa[:, piece] * (slope[:, piece] + far[:slab])
        flux[:, piece] = value
        store_rows(left_product(send[...], value), outs, piece)


def rim_matrix(table, weight, mask, block_matrix, own_blocks, high, low):
    width = block_matrix.shape[0]
    slots, blocks = table.shape
    for piece in chunks(mask.shape[1]):
        block = (piece.start + lax.broadcasted_iota(jnp.int32, (blocks, piece.stop - piece.start), 1)) // width
        pick = jnp.where(block == lax.broadcasted_iota(jnp.int32, block.shape, 0), 1.0, 0.0)
        spread_out = lambda rows: jnp.dot(
            rows, pick, precision=lax.Precision.HIGHEST, preferred_element_type=jnp.float32
        )
        index = spread_out(table[...].astype(jnp.float32))
        value = spread_out(weight[...]) * mask[:, piece]
        wide = jnp.concatenate([block_matrix[...]] * (block.shape[1] // width), axis=1)
        for received in range(high.shape[0] // width):
            hit = jnp.where(jnp.abs(index - (own_blocks + received)) < 0.5, value, 0.0)
            gain = jnp.sum(hit[1:slots], axis=0, keepdims=True)
            rows = slice(received * width, (received + 1) * width)
            high[rows, piece], low[rows, piece] = split(wide * gain)


def local_kernel(lookup, conductance, matrix, field, carried, flux, mask, spread, local, onward, *refs):
    out, slope, high, low, table, weight, rows_table, rows_weight, block_matrix, extended, gathered, sems = refs
    slab, nodes = field.shape
    tables = [(lookup, table), (conductance, weight), (lookup, rows_table), (conductance, rows_weight)]
    got = load([*tables, (matrix, block_matrix)], sems)
    for piece in chunks(nodes):
        step = axial_step * mask[:, piece] * left_product(local[...], flux[:, piece])
        values = jnp.concatenate([field[:, piece] + step[:slab], carried[:, piece] + step[slab:]], axis=0)
        out[:, piece] = values
        own = left_product(onward[...], values)
        for tile in range(piece.start // lanes, piece.stop // lanes):
            fill(extended, tile, own[:, tile * lanes - piece.start : (tile + 1) * lanes - piece.start])
    clear_from(extended, 2 * (nodes // lanes))
    for copy in got:
        copy.wait()
    for piece, values in conducted(table, weight, mask, spread, extended, gathered, chunks(nodes)):
        slope[:, piece] = values
    rim_matrix(rows_table, rows_weight, mask, block_matrix, nodes // block_matrix.shape[0], high, low)


def rim_kernel(spans, exported, base, mask, far, *refs):
    got, (first, second, faces, sems) = refs[: spans - 1], refs[spans - 1 :]
    (copy,) = load([(exported, faces)], sems)
    copy.wait()
    for side, out in zip(sides(), (first, second)):
        rows = jnp.concatenate([take_face(ref, faces, side) for ref in got], axis=0)
        out[...] = take_face(base, faces, side) + axial_step * take_face(mask, faces, side) * left_product(far[...], rows)


def close_kernel(spans, lookup, conductance, slope, mask, spread, onward_far, *refs):
    got, (out, table, weight, extended, gathered, sems) = refs[: spans - 1], refs[spans - 1 :]
    nodes = out.shape[1]
    copies = load([(lookup, table), (conductance, weight)], sems)
    for tile in range(nodes // lanes):
        fill(extended, tile, mask[:, tile_at(tile)] * stacked(got, tile_at(tile)))
    clear_from(extended, 2 * (nodes // lanes))
    for copy in copies:
        copy.wait()
    for piece, values in conducted(table, weight, mask, spread, extended, gathered, chunks(nodes)):
        out[:, piece] = slope[:, piece] + left_product(onward_far[...], values)


def second_kernel(slope, first, second, high, low, kappa, onward, *refs):
    sends, flux, outs = refs[:2], refs[2], refs[3:]
    slab, nodes = slope.shape
    rim = first.shape[1]
    received = []
    for side, values in zip(sides(), (first, second)):
        top, bottom = split(left_product(onward[...], values[...]))
        received.append((pl.ds(pl.multiple_of(side * rim, rim), rim), top, jnp.concatenate([top, bottom], axis=0)))
    for piece in chunks(nodes):
        total = slope[:, piece]
        for rows, top, both in received:
            main = jnp.dot(both, high[rows, piece], preferred_element_type=jnp.float32)
            total = total + (main[:slab] + main[slab:])
            total = total + jnp.dot(top, low[rows, piece], preferred_element_type=jnp.float32)
        value = kappa[:, piece] * total
        flux[:, piece] = value
        half = piece.start // (nodes // 2)
        store_folded(left_product(sends[half][...], value), outs, piece, nodes)


def rest_kernel(spans, lookup, conductance, base, flux, first, second, mask, spread, local, far, *refs):
    got, (out, table, weight, extended, gathered, sems) = refs[: spans - 1], refs[spans - 1 :]
    slab, nodes = flux.shape
    copies = load([(lookup, table), (conductance, weight)], sems)
    for piece in chunks(nodes):
        own = base[:slab, piece] + axial_step * mask[:, piece] * left_product(far[:slab], stacked(got, piece))
        for tile in range(piece.start // lanes, piece.stop // lanes):
            fill(extended, tile, own[:, tile * lanes - piece.start : (tile + 1) * lanes - piece.start])
    fill_rim(extended, first[:slab], second[:slab])
    for copy in copies:
        copy.wait()
    for piece, values in conducted(table, weight, mask, spread, extended, gathered, chunks(nodes)):
        out[:, piece] = values + axial_step * mask[:, piece] * left_product(local[:slab], flux[:, piece])


def last_kernel(spans, base, mask, *refs):
    fars, got, (out, values, sems) = refs[:2], refs[2 : spans + 1], refs[spans + 1 :]
    slab, nodes = base.shape
    copies = []
    for i, piece in enumerate(chunks(nodes)):
        half, rows = load_folded(got, piece, nodes)
        values[:, piece] = base[:, piece] + axial_step * mask[:, piece] * left_product(fars[half][:slab], rows)
        part = pl.ds(piece.start, piece.stop - piece.start)
        copies.append(pltpu.make_async_copy(values.at[:, part], out.at[:, part], sems.at[i]))
        copies[-1].start()
    for copy in copies:
        copy.wait()


def in_place(array):
    return pltpu.with_memory_space_constraint(array, pltpu.HBM)


def call(kernel, far, near, outs, scratch=(), flops=0, name=None, scalars=(), out_space=pltpu.VMEM):
    outs = [out if isinstance(out, jax.ShapeDtypeStruct) else jax.ShapeDtypeStruct(out, jnp.float32) for out in outs]
    size = sum(4 * array.size for array in [*near, *outs])
    spaces = [(scalars, pltpu.SMEM), (far, pltpu.HBM), (near, pltpu.VMEM)]
    return pl.pallas_call(
        kernel,
        in_specs=[pl.BlockSpec(memory_space=space) for arrays, space in spaces for _ in arrays],
        out_specs=[pl.BlockSpec(memory_space=out_space)] * len(outs),
        out_shape=outs,
        scratch_shapes=list(scratch),
        compiler_params=pltpu.CompilerParams(vmem_limit_bytes=24 * 2**20),
        cost_estimate=pl.CostEstimate(flops=flops, bytes_accessed=size, transcendentals=0),
        name=name,
    )(*scalars, *[in_place(array) for array in far], *near)


def trade_faces(first, second):
    count = lax.axis_size("xs")
    swap = lambda start: [pair for i in range(start, count - 1, 2) for pair in ((i, i + 1), (i + 1, i))]
    return lax.ppermute(first, "xs", swap(1)), lax.ppermute(second, "xs", swap(0))


def trade_slabs(parts):
    count = lax.axis_size("hgt")
    return [lax.ppermute(part, "hgt", [(i, i ^ x) for i in range(count)]) for x, part in zip(turns(count), parts)]


def slab_body(factors, field, kappa, lookup, conductance, exported, totals, pipe, matrix):
    slab, nodes = field.shape
    spans = lax.axis_size("hgt")
    faces = exported.shape[1:]
    rim = faces[1] * matrix.shape[0]
    tables = [lookup.T, conductance.T]
    exported = exported.reshape(faces)
    tall = slab + carried_rows
    tiles = (nodes + 2 * rim) // lanes + 1
    sent = [(8, rank // 8 * nodes + (rank % 8 > 0) * nodes // 2) for rank in factors["ranks"]]
    sent_joint = [(rank, nodes) for rank in factors["joint_ranks"]]
    whole = (slab, nodes)
    work = 2 * nodes * slab * slab

    def conduct_scratch(height, copies=2, more=()):
        return [
            pltpu.SMEM(tables[0].shape, jnp.int32),
            pltpu.SMEM(tables[1].shape, jnp.float32),
            *more,
            pltpu.VMEM((2 * tiles, height, lanes), jnp.float32),
            pltpu.VMEM((height, nodes), jnp.float32),
            pltpu.SemaphoreType.DMA((copies,)),
        ]

    face_scratch = pltpu.SMEM(faces, jnp.int32)
    first, second = call(
        faces_kernel,
        [exported, field],
        [],
        [(slab, rim)] * 2,
        [face_scratch, pltpu.VMEM((slab, nodes // 2), jnp.float32), pltpu.SemaphoreType.DMA((2,))],
        name="faces",
    )
    left, right = trade_faces(first, second)
    names = ["send_rows"] + sorted(name for name in factors["sets"] if name != "send_rows")
    stacks = [jnp.asarray(factors["sets"][name]) for name in names]
    height = stacks[0].shape[1]
    spread = jax.ShapeDtypeStruct((6 * lanes, 2 * lanes), jnp.bfloat16)
    mask, spread, state, moments, *own = call(
        functools.partial(prepare_kernel, len(stacks)),
        [pipe.reshape(1, nodes), matrix, field, *stacks],
        [],
        [(1, nodes), spread, whole, (height, nodes)]
        + [jax.ShapeDtypeStruct(stack.shape[1:], jnp.bfloat16) for stack in stacks],
        [
            pltpu.VMEM((1, nodes), jnp.int32),
            pltpu.VMEM(matrix.shape, jnp.float32),
            pltpu.VMEM(whole, jnp.float32),
            pltpu.SemaphoreType.DMA((3 + len(stacks),)),
        ],
        work,
        "prepare",
        [totals],
    )
    own = dict(zip(names, own))
    sends = [own["send_half0"], own["send_half1"]]
    fars = [own["far_half0"], own["far_half1"]]
    parts = call(
        moments_kernel, tables, [moments, left, right, mask, spread, own["send_rows"]], sent, conduct_scratch(height), name="moments"
    )
    parts = trade_slabs(parts)
    state, slope = call(
        first_kernel,
        tables,
        [state, left, right, mask, spread, own["local"]],
        [whole, whole],
        conduct_scratch(slab),
        2 * work,
        "first",
    )
    flux, carried, *joint = call(
        functools.partial(flux_kernel, spans),
        [],
        [slope, *parts, kappa, own["send_joint"], *fars],
        [whole, (carried_rows, nodes)] + sent_joint,
        name="flux",
    )
    joint = trade_slabs(joint)
    half_matrix = jax.ShapeDtypeStruct((2 * rim, nodes), jnp.bfloat16)
    base, slope, high, low = call(
        local_kernel,
        [*tables, matrix],
        [state, carried, flux, mask, spread, own["local"], own["onward"]],
        [(tall, nodes), whole, half_matrix, half_matrix],
        conduct_scratch(
            slab,
            5,
            [
                pltpu.VMEM(tables[0].shape, jnp.int32),
                pltpu.VMEM(tables[1].shape, jnp.float32),
                pltpu.VMEM(matrix.shape, jnp.float32),
            ],
        ),
        4 * work,
        "local",
    )
    first, second = call(
        functools.partial(rim_kernel, spans),
        [exported],
        [base, mask, own["far_joint"], *joint],
        [(tall, rim)] * 2,
        [face_scratch, pltpu.SemaphoreType.DMA((1,))],
        name="rim",
    )
    left, right = trade_faces(first, second)
    (slope,) = call(
        functools.partial(close_kernel, spans),
        tables,
        [slope, mask, spread, own["onward_far"], *joint],
        [whole],
        conduct_scratch(sum(rank for rank, _ in sent_joint)),
        work,
        "close",
    )
    flux, *parts = call(
        second_kernel,
        [],
        [slope, left, right, high, low, kappa, own["onward"], *sends],
        [whole] + sent,
        name="second",
    )
    parts = trade_slabs(parts)
    (state,) = call(
        functools.partial(rest_kernel, spans),
        tables,
        [base, flux, left, right, mask, spread, own["local"], own["far_joint"], *joint],
        [whole],
        conduct_scratch(slab),
        2 * work,
        "rest",
    )
    (state,) = call(
        functools.partial(last_kernel, spans),
        [],
        [state, mask, *fars, *parts],
        [whole],
        [pltpu.VMEM(whole, jnp.float32), pltpu.SemaphoreType.DMA((len(chunks(nodes)),))],
        name="last",
        out_space=pltpu.HBM,
    )
    return state


def padded_2(cells, sides, width):
    for axis, dim in sides:
        count = lax.axis_size(axis)
        ends = count - 1
        head = lax.slice_in_dim(cells, 0, width, axis=dim)
        tail = lax.slice_in_dim(cells, cells.shape[dim] - width, cells.shape[dim], axis=dim)
        cells = jnp.concatenate(
            [
                lax.ppermute(tail, axis, [(i, (i + 1) % count) for i in range(ends)]),
                cells,
                lax.ppermute(head, axis, [((i + 1) % count, i) for i in range(ends)]),
            ],
            axis=dim,
        )
    return cells


def cheb_matrix(order):
    index = jnp.arange(order)
    row_f = index[:, None].astype(jnp.float32)
    col_f = index[None, :].astype(jnp.float32)
    angle = math.pi / (2.0 * (order - 1))
    difference = -2.0 * jnp.sin((row_f + col_f) * angle) * jnp.sin((row_f - col_f) * angle)
    ends = (index == 0) | (index == order - 1)
    weight = jnp.where(ends, 2.0, 1.0).astype(jnp.float32)
    parity = jnp.where((index[:, None] + index[None, :]) % 2 == 0, 1.0, -1.0).astype(jnp.float32)
    off_diag = index[:, None] != index[None, :]
    safe_diff = jnp.where(off_diag, difference, jnp.float32(1.0))
    entries = jnp.where(
        off_diag, weight[:, None] / weight[None, :] * parity / safe_diff, jnp.float32(0.0)
    )
    entries = entries - jnp.diag(jnp.sum(entries, axis=1))
    mirror = jnp.minimum(index, order - 1 - index).astype(jnp.float32)
    sine = jnp.sin(mirror * (2.0 * angle))
    return -sine[:, None] * entries / (order - 1)


def slot_sum(source, indices, boundary_entry_conductances, total):
    for slot_index in range(indices.shape[1]):
        picked = source[:, indices[:, slot_index], :]
        total = total + boundary_entry_conductances[None, :, slot_index, None] * picked
    return total


def conduct(
    present_solution,
    boundary_group_lookup,
    boundary_entry_conductances,
    exported_boundary_groups,
    spread,
    slab_mask,
    width,
):
    height, plane_vertices = present_solution.shape
    blocks = plane_vertices // width
    face_count = exported_boundary_groups.shape[2]
    blocked = present_solution.reshape(height, blocks, width)
    outgoing = jnp.concatenate(
        [
            blocked[:, exported_boundary_groups[0, 0], :],
            blocked[:, exported_boundary_groups[0, 1], :],
        ],
        axis=1,
    )
    outgoing = outgoing.reshape(height, 2 * face_count * width)
    rim_width = face_count * width
    padded = padded_2(outgoing, (("xs", 1),), rim_width)
    from_left = padded[:, :rim_width].reshape(height, face_count, width)
    from_right = padded[:, padded.shape[1] - rim_width :].reshape(height, face_count, width)
    empty = jnp.zeros((height, 1, width), jnp.float32)
    gathered = jnp.zeros((height, blocks, width), jnp.float32)
    extended = jnp.concatenate([blocked, from_left, from_right, empty], axis=1)
    gathered = slot_sum(extended, boundary_group_lookup, boundary_entry_conductances, gathered)
    coupled = jnp.dot(
        gathered.reshape(-1, spread.shape[0]),
        spread,
        precision=lax.Precision.HIGHEST,
        preferred_element_type=jnp.float32,
    ).reshape(height, plane_vertices)
    return present_solution + slab_mask[None, :] * coupled


def axial(column_field, column_kappa, operator, column_mask):
    slope = jnp.dot(
        operator, column_field, precision=lax.Precision.HIGHEST, preferred_element_type=jnp.float32
    )
    second = jnp.dot(
        operator,
        column_kappa * slope,
        precision=lax.Precision.HIGHEST,
        preferred_element_type=jnp.float32,
    )
    return column_field + axial_step * column_mask[None, :] * second


def to_columns(moved):
    return lax.all_to_all(moved, "hgt", split_axis=1, concat_axis=0, tiled=True)


def to_slabs(result):
    return lax.all_to_all(result, "hgt", split_axis=0, concat_axis=1, tiled=True)


def column_body(
    thermal_field,
    thermal_diffusivity,
    boundary_group_lookup,
    boundary_entry_conductances,
    exported_boundary_groups,
    domain_group_totals,
    pipe_cavity_indicator,
    boundary_vertex_matrix,
):
    layer_sample_number, plane_vertices = thermal_field.shape
    width = boundary_vertex_matrix.shape[0]
    group_size = max(1, 128 // width)
    spread = jnp.kron(jnp.eye(group_size, dtype=jnp.float32), boundary_vertex_matrix)
    block_ids = jnp.arange(plane_vertices) // width
    live_groups = block_ids < domain_group_totals[0]
    slab_mask = jnp.where(live_groups & (pipe_cavity_indicator == 0), 1.0, 0.0).astype(jnp.float32)
    spans = lax.axis_size("hgt")
    column_count = plane_vertices // spans
    column_start = lax.axis_index("hgt") * column_count
    column_mask = lax.dynamic_slice_in_dim(slab_mask, column_start, column_count, 0)
    operator = cheb_matrix(layer_sample_number * spans)
    present_solution = jnp.where(live_groups[None, :], thermal_field, jnp.float32(0.0))
    moved = conduct(
        present_solution,
        boundary_group_lookup,
        boundary_entry_conductances,
        exported_boundary_groups,
        spread,
        slab_mask,
        width,
    )
    column_field, kappa_fixed = (
        lax.all_to_all(moved, "hgt", split_axis=1, concat_axis=0, tiled=True),
        lax.all_to_all(thermal_diffusivity, "hgt", split_axis=1, concat_axis=0, tiled=True),
    )
    result = axial(column_field, kappa_fixed, operator, column_mask)
    present_solution = to_slabs(result)
    moved = conduct(
        present_solution,
        boundary_group_lookup,
        boundary_entry_conductances,
        exported_boundary_groups,
        spread,
        slab_mask,
        width,
    )
    result = axial(to_columns(moved), kappa_fixed, operator, column_mask)
    present_solution = to_slabs(result)
    return present_solution


def body(field, kappa, lookup, conductance, exported, totals, pipe, matrix):
    spans = lax.axis_size("hgt")
    factors = slab_factors(field.shape[0] * spans, spans)
    args = (field, kappa, lookup, conductance, exported, totals, pipe, matrix)
    if factors is None or 2 * matrix.shape[0] != lanes:
        return column_body(*args)
    return slab_body(factors, *args)


def solution(mesh):
    in_specs = (
        P("hgt", ("grp", "xs")),
        P("hgt", ("grp", "xs")),
        P("xs", None),
        P("xs", None),
        P("xs", None, None),
        P("xs"),
        P("xs"),
        P(),
    )
    out_specs = P("hgt", ("grp", "xs"))
    return jax.shard_map(body, mesh=mesh, in_specs=in_specs, out_specs=out_specs, check_vma=False)
```

```python
import functools
import math

import ml_dtypes
import numpy as np
import jax
import jax.numpy as jnp
from jax import lax
from jax.experimental import pallas as pl
from jax.experimental.pallas import tpu as pltpu
from jax.sharding import PartitionSpec as P

axial_step = 0.5
lanes = 128
near_rows = 12
far_rows = 4
joint_near_rows = 16
joint_far_rows = 8
carried_rows = 24


def cheb_exact(order):
    index = np.arange(order, dtype=np.float64)
    angle = math.pi / (2.0 * (order - 1))
    row, col = index[:, None], index[None, :]
    difference = -2.0 * np.sin((row + col) * angle) * np.sin((row - col) * angle)
    weight = np.ones(order)
    weight[0] = weight[-1] = 2.0
    parity = np.where((row + col) % 2 == 0, 1.0, -1.0)
    off_diag = row != col
    entries = np.where(
        off_diag, weight[:, None] / weight[None, :] * parity / np.where(off_diag, difference, 1.0), 0.0
    )
    entries = entries - np.diag(entries.sum(axis=1))
    sine = np.sin(np.minimum(index, order - 1 - index) * (2.0 * angle))
    return -sine[:, None] * entries / (order - 1)


def row_basis(block, rank):
    return np.linalg.svd(block, full_matrices=False)[2][:rank]


def halves(matrix):
    high = matrix.astype(ml_dtypes.bfloat16)
    return high, (matrix - high.astype(np.float64)).astype(ml_dtypes.bfloat16)


def pad_to(matrix, rows, cols):
    return np.pad(matrix, ((0, rows - matrix.shape[0]), (0, cols - matrix.shape[1])))


def round_up(size, step):
    return -(-size // step) * step


def as_left(matrix):
    high, low = halves(pad_to(matrix, matrix.shape[0], round_up(matrix.shape[1], 16)))
    return np.concatenate([high, high, low], axis=1)


def fold(rows, half, axis):
    whole = rows.shape[axis] // 8 * 8
    head, tail = np.split(rows, [whole], axis=axis)
    if not tail.shape[axis]:
        return head, tail
    zeros = np.zeros_like(tail)
    return head, np.concatenate([zeros, tail] if half else [tail, zeros], axis=axis)


def folded(parts, half, axis):
    pairs = [fold(part, half, axis) for part in parts]
    return np.concatenate([head for head, _ in pairs] + [tail for _, tail in pairs], axis=axis)


def turns(spans):
    return list(range(spans - 1, 0, -1))


@functools.lru_cache(maxsize=None)
def slab_factors(order, spans):
    slab = order // spans
    if spans & (spans - 1) or spans > 4 or slab < 128:
        return None
    full = cheb_exact(order)
    block = lambda s, t: full[s * slab : (s + 1) * slab, t * slab : (t + 1) * slab]
    near = {x: any(abs(s - (s ^ x)) == 1 for s in range(spans)) for x in turns(spans)}
    ranks = {x: near_rows if close else far_rows for x, close in near.items()}
    joint_ranks = {x: joint_near_rows if close else joint_far_rows for x, close in near.items()}
    first, joint = {}, {}
    carried, onward, left = {}, {}, {}
    for s in range(spans):
        others = [t for t in range(spans) if t != s]
        u, sigma, vt = np.linalg.svd(np.concatenate([block(s, t) for t in others], axis=1), full_matrices=False)
        left[s] = u[:, :carried_rows]
        rows = sigma[:carried_rows, None] * vt[:carried_rows]
        carried[s] = {t: rows[:, i * slab : (i + 1) * slab] for i, t in enumerate(others)}
        onward[s] = sum(carried[s][t] @ full[t * slab : (t + 1) * slab] for t in others)
        for t in others:
            first[s, t] = row_basis(block(s, t), ranks[s ^ t])
            joint[s, t] = row_basis(
                np.concatenate([block(s, t), onward[s][:, t * slab : (t + 1) * slab]], axis=0), joint_ranks[s ^ t]
            )
    sets = {}

    def add(name, matrix):
        sets.setdefault(name, []).append(as_left(matrix))

    for s in range(spans):
        partners = [s ^ x for x in turns(spans)]
        cut = lambda t: slice(t * slab, (t + 1) * slab)
        firsts = [np.concatenate([block(s, t), carried[s][t]], axis=0) @ first[s, t].T for t in partners]
        joints = [np.concatenate([block(s, t), onward[s][:, cut(t)]], axis=0) @ joint[s, t].T for t in partners]
        for half in range(2):
            add("send_half%d" % half, folded([first[t, s] for t in partners], half, 0))
            add("far_half%d" % half, folded(firsts, half, 1))
        add("send_rows", folded([first[t, s] for t in partners], 0, 0))
        add("send_joint", np.concatenate([joint[t, s] for t in partners], axis=0))
        joint_far = np.concatenate(joints, axis=1)
        add("far_joint", joint_far)
        add("onward_far", axial_step * np.concatenate([block(s, s), left[s]], axis=1) @ joint_far)
        add("local", np.concatenate([block(s, s), onward[s][:, cut(s)]], axis=0))
        add("onward", np.concatenate([block(s, s), left[s]], axis=1))
    return dict(
        ranks=list(ranks.values()), joint_ranks=list(joint_ranks.values()), sets={name: np.stack(parts) for name, parts in sets.items()}
    )


def split(values):
    high = values.astype(jnp.bfloat16)
    return high, (values - high.astype(jnp.float32)).astype(jnp.bfloat16)


def left_product(left, values):
    short = left.shape[1] // 3 - values.shape[0]
    if short:
        values = jnp.concatenate([values, jnp.zeros((short, values.shape[1]), jnp.float32)], axis=0)
    high, low = split(values)
    return jnp.dot(left, jnp.concatenate([high, low, high], axis=0), preferred_element_type=jnp.float32)


def right_product(values, right):
    high, low = split(values)
    return jnp.dot(jnp.concatenate([high, low, high], axis=1), right, preferred_element_type=jnp.float32)


def low_half():
    return lax.broadcasted_iota(jnp.int32, (1, lanes), 1) < lanes // 2


def tile_at(tile):
    return slice(tile * lanes, (tile + 1) * lanes)


def chunks(width):
    step = min(width, 512)
    return [slice(start, start + step) for start in range(0, width, step)]


def load(copies, sems):
    started = [pltpu.make_async_copy(source, target, sems.at[i]) for i, (source, target) in enumerate(copies)]
    for copy in started:
        copy.start()
    return started


def sides():
    first = 1 - lax.axis_index("xs") % 2
    return first, 1 - first


def take_face(source, exported, side):
    tiles = []
    for tile in range(exported.shape[1] // 2):
        parts = []
        for place in range(2):
            index = exported[side, 2 * tile + place]
            value = source[:, pl.ds(pl.multiple_of((index >> 1) * lanes, lanes), lanes)]
            parts.append(jnp.where(index & 1 == place, value, pltpu.roll(value, lanes // 2, 1)))
        tiles.append(jnp.where(low_half(), parts[0], parts[1]))
    return jnp.concatenate(tiles, axis=1)


def faces_kernel(exported, field, first, second, faces, near, sems):
    got = load([(exported, faces), (field.at[:, pl.ds(0, near.shape[1])], near)], sems)
    for copy in got:
        copy.wait()
    for side, out in zip(sides(), (first, second)):
        out[...] = take_face(near, faces, side)


def prepare_kernel(count, total, pipe, matrix, field, *refs):
    stacks, (mask, spread, state, moments), outs = refs[:count], refs[count : count + 4], refs[count + 4 : 2 * count + 4]
    holes, block_matrix, values, sems = refs[2 * count + 4 :]
    where = lax.axis_index("hgt")
    pairs = [(matrix, block_matrix), (pipe, holes), (field, values)]
    got = load(pairs + [(stack.at[where], out) for stack, out in zip(stacks, outs)], sems)
    got[0].wait()
    width = matrix.shape[0]
    size = spread.shape[1]
    wide = jnp.concatenate([block_matrix[...]] * (size // width), axis=1)
    tall = jnp.concatenate([wide] * (size // width), axis=0)
    row = lax.broadcasted_iota(jnp.int32, tall.shape, 0) // width
    col = lax.broadcasted_iota(jnp.int32, tall.shape, 1) // width
    high, low = split(jnp.where(row == col, tall, 0.0))
    spread[...] = jnp.concatenate([high, high, low], axis=0)
    got[1].wait()
    block = lax.broadcasted_iota(jnp.int32, mask.shape, 1) // width
    live = block < total[0]
    mask[...] = jnp.where(live & (holes[...] == 0), 1.0, 0.0).astype(jnp.float32)
    for copy in got[2:]:
        copy.wait()
    for piece in chunks(field.shape[1]):
        state[:, piece] = jnp.where(live[:, piece], values[:, piece], 0.0)
        moments[:, piece] = left_product(outs[0][...], state[:, piece])


def fill(extended, tile, value):
    extended[2 * tile] = value
    extended[2 * tile + 1] = pltpu.roll(value, lanes // 2, 1)


def fill_own(extended, own):
    for tile in range(own.shape[1] // lanes):
        fill(extended, tile, own[:, tile_at(tile)])


def clear_from(extended, start):
    for entry in range(start, extended.shape[0]):
        extended[entry] = jnp.zeros(extended.shape[1:], jnp.float32)


def fill_rim(extended, first, second):
    rim = first.shape[1] // lanes
    start = extended.shape[0] // 2 - 1 - 2 * rim
    for side, values in zip(sides(), (first, second)):
        for tile in range(rim):
            fill(extended, start + side * rim + tile, values[:, tile_at(tile)])
    clear_from(extended, extended.shape[0] - 2)


def conducted(lookup, conductance, mask, spread, extended, gathered, pieces):
    half = low_half()
    per = spread.shape[1] // lanes
    for piece in pieces:
        start = piece.start // lanes
        for tile in range(start, piece.stop // lanes):
            low, high = 2 * tile, 2 * tile + 1
            total = jnp.where(half, conductance[0, low], conductance[0, high]) * extended[2 * tile]
            for slot in range(1, lookup.shape[0]):
                one, two = lookup[slot, low], lookup[slot, high]
                value = jnp.where(half, extended[one], extended[two ^ 1])
                total = total + jnp.where(half, conductance[slot, low], conductance[slot, high]) * value
            gathered[:, tile_at(tile)] = total
        moved = []
        for tile in range(start, piece.stop // lanes, per):
            part = slice(tile * lanes, (tile + per) * lanes)
            own = jnp.concatenate([extended[2 * (tile + i)] for i in range(per)], axis=1)
            moved.append(own + mask[:, part] * right_product(gathered[:, part], spread[...]))
        yield piece, jnp.concatenate(moved, axis=1)


def store_rows(moved, outs, piece):
    start = 0
    for out in outs:
        out[:, piece] = moved[start : start + out.shape[0]]
        start += out.shape[0]


def stacked(refs, piece):
    return jnp.concatenate([ref[:, piece] for ref in refs], axis=0)


def folded_views(refs, piece, nodes):
    half = piece.start // (nodes // 2)
    heads = [(ref, piece) for ref in refs if ref.shape[1] >= nodes]
    tails = []
    for ref in refs:
        start = (nodes if ref.shape[1] >= nodes else 0) + piece.start - half * (nodes // 2)
        if ref.shape[1] != nodes:
            tails.append((ref, slice(start, start + piece.stop - piece.start)))
    return half, heads, tails


def store_folded(moved, refs, piece, nodes):
    half, heads, tails = folded_views(refs, piece, nodes)
    for i, (ref, part) in enumerate(heads + tails):
        value = moved[8 * i : 8 * i + 8]
        ref[:, part] = ref[:, part] + value if half and i >= len(heads) else value


def load_folded(refs, piece, nodes):
    half, heads, tails = folded_views(refs, piece, nodes)
    return half, jnp.concatenate([ref[:, part] for ref, part in heads + tails], axis=0)


def moments_kernel(lookup, conductance, moments, first, second, mask, spread, send, *refs):
    outs, (table, weight, extended, gathered, sems) = refs[:-5], refs[-5:]
    nodes = moments.shape[1]
    got = load([(lookup, table), (conductance, weight)], sems)
    fill_own(extended, moments)
    fill_rim(extended, left_product(send[...], first[...]), left_product(send[...], second[...]))
    for copy in got:
        copy.wait()
    whole = 8 * sum(out.shape[1] >= nodes for out in outs)
    for piece, values in conducted(table, weight, mask, spread, extended, gathered, chunks(nodes)):
        if piece.start >= nodes // 2:
            tails = [pltpu.roll(values[i : i + 8], 4, 0) for i in range(whole, values.shape[0], 8)]
            values = jnp.concatenate([values[:whole]] + tails, axis=0)
        store_folded(values, outs, piece, nodes)


def first_kernel(lookup, conductance, field, first, second, mask, spread, local, out, slope, *scratch):
    table, weight, extended, gathered, sems = scratch
    slab = field.shape[0]
    got = load([(lookup, table), (conductance, weight)], sems)
    fill_own(extended, field)
    fill_rim(extended, first, second)
    for copy in got:
        copy.wait()
    for piece, values in conducted(table, weight, mask, spread, extended, gathered, chunks(field.shape[1])):
        out[:, piece] = values
        slope[:, piece] = left_product(local[:slab], values)


def flux_kernel(spans, slope, *refs):
    got, (kappa, send), fars, (flux, carried), outs = (
        refs[: spans - 1],
        refs[spans - 1 : spans + 1],
        refs[spans + 1 : spans + 3],
        refs[spans + 3 : spans + 5],
        refs[spans + 5 :],
    )
    slab, nodes = slope.shape
    for piece in chunks(nodes):
        half, rows = load_folded(got, piece, nodes)
        far = left_product(fars[half][...], rows)
        carried[:, piece] = far[slab:]
        value = kappa[:, piece] * (slope[:, piece] + far[:slab])
        flux[:, piece] = value
        store_rows(left_product(send[...], value), outs, piece)


def rim_matrix(table, weight, mask, block_matrix, own_blocks, high, low):
    width = block_matrix.shape[0]
    slots, blocks = table.shape
    for piece in chunks(mask.shape[1]):
        block = (piece.start + lax.broadcasted_iota(jnp.int32, (blocks, piece.stop - piece.start), 1)) // width
        pick = jnp.where(block == lax.broadcasted_iota(jnp.int32, block.shape, 0), 1.0, 0.0)
        spread_out = lambda rows: jnp.dot(
            rows, pick, precision=lax.Precision.HIGHEST, preferred_element_type=jnp.float32
        )
        index = spread_out(table[...].astype(jnp.float32))
        value = spread_out(weight[...]) * mask[:, piece]
        wide = jnp.concatenate([block_matrix[...]] * (block.shape[1] // width), axis=1)
        for received in range(high.shape[0] // width):
            hit = jnp.where(jnp.abs(index - (own_blocks + received)) < 0.5, value, 0.0)
            gain = jnp.sum(hit[1:slots], axis=0, keepdims=True)
            rows = slice(received * width, (received + 1) * width)
            high[rows, piece], low[rows, piece] = split(wide * gain)


def local_kernel(lookup, conductance, matrix, field, carried, flux, mask, spread, local, onward, *refs):
    out, slope, high, low, table, weight, rows_table, rows_weight, block_matrix, extended, gathered, sems = refs
    slab, nodes = field.shape
    tables = [(lookup, table), (conductance, weight), (lookup, rows_table), (conductance, rows_weight)]
    got = load([*tables, (matrix, block_matrix)], sems)
    for piece in chunks(nodes):
        step = axial_step * mask[:, piece] * left_product(local[...], flux[:, piece])
        values = jnp.concatenate([field[:, piece] + step[:slab], carried[:, piece] + step[slab:]], axis=0)
        out[:, piece] = values
        own = left_product(onward[...], values)
        for tile in range(piece.start // lanes, piece.stop // lanes):
            fill(extended, tile, own[:, tile * lanes - piece.start : (tile + 1) * lanes - piece.start])
    clear_from(extended, 2 * (nodes // lanes))
    for copy in got:
        copy.wait()
    for piece, values in conducted(table, weight, mask, spread, extended, gathered, chunks(nodes)):
        slope[:, piece] = values
    rim_matrix(rows_table, rows_weight, mask, block_matrix, nodes // block_matrix.shape[0], high, low)


def rim_kernel(spans, exported, base, mask, far, *refs):
    got, (first, second, faces, sems) = refs[: spans - 1], refs[spans - 1 :]
    (copy,) = load([(exported, faces)], sems)
    copy.wait()
    for side, out in zip(sides(), (first, second)):
        rows = jnp.concatenate([take_face(ref, faces, side) for ref in got], axis=0)
        out[...] = take_face(base, faces, side) + axial_step * take_face(mask, faces, side) * left_product(far[...], rows)


def close_kernel(spans, lookup, conductance, slope, mask, spread, onward_far, *refs):
    got, (out, table, weight, extended, gathered, sems) = refs[: spans - 1], refs[spans - 1 :]
    nodes = out.shape[1]
    copies = load([(lookup, table), (conductance, weight)], sems)
    for tile in range(nodes // lanes):
        fill(extended, tile, mask[:, tile_at(tile)] * stacked(got, tile_at(tile)))
    clear_from(extended, 2 * (nodes // lanes))
    for copy in copies:
        copy.wait()
    for piece, values in conducted(table, weight, mask, spread, extended, gathered, chunks(nodes)):
        out[:, piece] = slope[:, piece] + left_product(onward_far[...], values)


def second_kernel(slope, first, second, high, low, kappa, onward, *refs):
    sends, flux, outs = refs[:2], refs[2], refs[3:]
    slab, nodes = slope.shape
    rim = first.shape[1]
    received = []
    for side, values in zip(sides(), (first, second)):
        top, bottom = split(left_product(onward[...], values[...]))
        received.append((pl.ds(pl.multiple_of(side * rim, rim), rim), top, jnp.concatenate([top, bottom], axis=0)))
    for piece in chunks(nodes):
        total = slope[:, piece]
        for rows, top, both in received:
            main = jnp.dot(both, high[rows, piece], preferred_element_type=jnp.float32)
            total = total + (main[:slab] + main[slab:])
            total = total + jnp.dot(top, low[rows, piece], preferred_element_type=jnp.float32)
        value = kappa[:, piece] * total
        flux[:, piece] = value
        half = piece.start // (nodes // 2)
        store_folded(left_product(sends[half][...], value), outs, piece, nodes)


def rest_kernel(spans, lookup, conductance, base, flux, first, second, mask, spread, local, far, *refs):
    got, (out, table, weight, extended, gathered, sems) = refs[: spans - 1], refs[spans - 1 :]
    slab, nodes = flux.shape
    copies = load([(lookup, table), (conductance, weight)], sems)
    for piece in chunks(nodes):
        own = base[:slab, piece] + axial_step * mask[:, piece] * left_product(far[:slab], stacked(got, piece))
        for tile in range(piece.start // lanes, piece.stop // lanes):
            fill(extended, tile, own[:, tile * lanes - piece.start : (tile + 1) * lanes - piece.start])
    fill_rim(extended, first[:slab], second[:slab])
    for copy in copies:
        copy.wait()
    for piece, values in conducted(table, weight, mask, spread, extended, gathered, chunks(nodes)):
        out[:, piece] = values + axial_step * mask[:, piece] * left_product(local[:slab], flux[:, piece])


def last_kernel(spans, base, mask, *refs):
    fars, got, (out, values, sems) = refs[:2], refs[2 : spans + 1], refs[spans + 1 :]
    slab, nodes = base.shape
    copies = []
    for i, piece in enumerate(chunks(nodes)):
        half, rows = load_folded(got, piece, nodes)
        values[:, piece] = base[:, piece] + axial_step * mask[:, piece] * left_product(fars[half][:slab], rows)
        part = pl.ds(piece.start, piece.stop - piece.start)
        copies.append(pltpu.make_async_copy(values.at[:, part], out.at[:, part], sems.at[i]))
        copies[-1].start()
    for copy in copies:
        copy.wait()


def in_place(array):
    return pltpu.with_memory_space_constraint(array, pltpu.HBM)


def call(kernel, far, near, outs, scratch=(), flops=0, name=None, scalars=(), out_space=pltpu.VMEM):
    outs = [out if isinstance(out, jax.ShapeDtypeStruct) else jax.ShapeDtypeStruct(out, jnp.float32) for out in outs]
    size = sum(4 * array.size for array in [*near, *outs])
    spaces = [(scalars, pltpu.SMEM), (far, pltpu.HBM), (near, pltpu.VMEM)]
    return pl.pallas_call(
        kernel,
        in_specs=[pl.BlockSpec(memory_space=space) for arrays, space in spaces for _ in arrays],
        out_specs=[pl.BlockSpec(memory_space=out_space)] * len(outs),
        out_shape=outs,
        scratch_shapes=list(scratch),
        compiler_params=pltpu.CompilerParams(vmem_limit_bytes=24 * 2**20),
        cost_estimate=pl.CostEstimate(flops=flops, bytes_accessed=size, transcendentals=0),
        name=name,
    )(*scalars, *[in_place(array) for array in far], *near)


def trade_faces(first, second):
    count = lax.axis_size("xs")
    swap = lambda start: [pair for i in range(start, count - 1, 2) for pair in ((i, i + 1), (i + 1, i))]
    return lax.ppermute(first, "xs", swap(0)), lax.ppermute(second, "xs", swap(1))


def trade_slabs(parts):
    count = lax.axis_size("hgt")
    return [lax.ppermute(part, "hgt", [(i, i ^ x) for i in range(count)]) for x, part in zip(turns(count), parts)]


def slab_body(factors, field, kappa, lookup, conductance, exported, totals, pipe, matrix):
    slab, nodes = field.shape
    spans = lax.axis_size("hgt")
    faces = exported.shape[1:]
    rim = faces[1] * matrix.shape[0]
    tables = [lookup.T, conductance.T]
    exported = exported.reshape(faces)
    tall = slab + carried_rows
    tiles = (nodes + 2 * rim) // lanes + 1
    sent = [(8, rank // 8 * nodes + (rank % 8 > 0) * nodes // 2) for rank in factors["ranks"]]
    sent_joint = [(rank, nodes) for rank in factors["joint_ranks"]]
    whole = (slab, nodes)
    work = 2 * nodes * slab * slab

    def conduct_scratch(height, copies=2, more=()):
        return [
            pltpu.SMEM(tables[0].shape, jnp.int32),
            pltpu.SMEM(tables[1].shape, jnp.float32),
            *more,
            pltpu.VMEM((2 * tiles, height, lanes), jnp.float32),
            pltpu.VMEM((height, nodes), jnp.float32),
            pltpu.SemaphoreType.DMA((copies,)),
        ]

    face_scratch = pltpu.SMEM(faces, jnp.int32)
    first, second = call(
        faces_kernel,
        [exported, field],
        [],
        [(slab, rim)] * 2,
        [face_scratch, pltpu.VMEM((slab, nodes // 2), jnp.float32), pltpu.SemaphoreType.DMA((2,))],
        name="faces",
    )
    left, right = trade_faces(first, second)
    names = ["send_rows"] + sorted(name for name in factors["sets"] if name != "send_rows")
    stacks = [jnp.asarray(factors["sets"][name]) for name in names]
    height = stacks[0].shape[1]
    spread = jax.ShapeDtypeStruct((6 * lanes, 2 * lanes), jnp.bfloat16)
    mask, spread, state, moments, *own = call(
        functools.partial(prepare_kernel, len(stacks)),
        [pipe.reshape(1, nodes), matrix, field, *stacks],
        [],
        [(1, nodes), spread, whole, (height, nodes)]
        + [jax.ShapeDtypeStruct(stack.shape[1:], jnp.bfloat16) for stack in stacks],
        [
            pltpu.VMEM((1, nodes), jnp.int32),
            pltpu.VMEM(matrix.shape, jnp.float32),
            pltpu.VMEM(whole, jnp.float32),
            pltpu.SemaphoreType.DMA((3 + len(stacks),)),
        ],
        work,
        "prepare",
        [totals],
    )
    own = dict(zip(names, own))
    sends = [own["send_half0"], own["send_half1"]]
    fars = [own["far_half0"], own["far_half1"]]
    parts = call(
        moments_kernel, tables, [moments, left, right, mask, spread, own["send_rows"]], sent, conduct_scratch(height), name="moments"
    )
    parts = trade_slabs(parts)
    state, slope = call(
        first_kernel,
        tables,
        [state, left, right, mask, spread, own["local"]],
        [whole, whole],
        conduct_scratch(slab),
        2 * work,
        "first",
    )
    flux, carried, *joint = call(
        functools.partial(flux_kernel, spans),
        [],
        [slope, *parts, kappa, own["send_joint"], *fars],
        [whole, (carried_rows, nodes)] + sent_joint,
        name="flux",
    )
    joint = trade_slabs(joint)
    half_matrix = jax.ShapeDtypeStruct((2 * rim, nodes), jnp.bfloat16)
    base, slope, high, low = call(
        local_kernel,
        [*tables, matrix],
        [state, carried, flux, mask, spread, own["local"], own["onward"]],
        [(tall, nodes), whole, half_matrix, half_matrix],
        conduct_scratch(
            slab,
            5,
            [
                pltpu.VMEM(tables[0].shape, jnp.int32),
                pltpu.VMEM(tables[1].shape, jnp.float32),
                pltpu.VMEM(matrix.shape, jnp.float32),
            ],
        ),
        4 * work,
        "local",
    )
    first, second = call(
        functools.partial(rim_kernel, spans),
        [exported],
        [base, mask, own["far_joint"], *joint],
        [(tall, rim)] * 2,
        [face_scratch, pltpu.SemaphoreType.DMA((1,))],
        name="rim",
    )
    left, right = trade_faces(first, second)
    (slope,) = call(
        functools.partial(close_kernel, spans),
        tables,
        [slope, mask, spread, own["onward_far"], *joint],
        [whole],
        conduct_scratch(sum(rank for rank, _ in sent_joint)),
        work,
        "close",
    )
    flux, *parts = call(
        second_kernel,
        [],
        [slope, left, right, high, low, kappa, own["onward"], *sends],
        [whole] + sent,
        name="second",
    )
    parts = trade_slabs(parts)
    (state,) = call(
        functools.partial(rest_kernel, spans),
        tables,
        [base, flux, left, right, mask, spread, own["local"], own["far_joint"], *joint],
        [whole],
        conduct_scratch(slab),
        2 * work,
        "rest",
    )
    (state,) = call(
        functools.partial(last_kernel, spans),
        [],
        [state, mask, *fars, *parts],
        [whole],
        [pltpu.VMEM(whole, jnp.float32), pltpu.SemaphoreType.DMA((len(chunks(nodes)),))],
        name="last",
        out_space=pltpu.HBM,
    )
    return state


def padded_2(cells, sides, width):
    for axis, dim in sides:
        count = lax.axis_size(axis)
        ends = count - 1
        head = lax.slice_in_dim(cells, 0, width, axis=dim)
        tail = lax.slice_in_dim(cells, cells.shape[dim] - width, cells.shape[dim], axis=dim)
        cells = jnp.concatenate(
            [
                lax.ppermute(tail, axis, [(i, (i + 1) % count) for i in range(ends)]),
                cells,
                lax.ppermute(head, axis, [((i + 1) % count, i) for i in range(ends)]),
            ],
            axis=dim,
        )
    return cells


def cheb_matrix(order):
    index = jnp.arange(order)
    row_f = index[:, None].astype(jnp.float32)
    col_f = index[None, :].astype(jnp.float32)
    angle = math.pi / (2.0 * (order - 1))
    difference = -2.0 * jnp.sin((row_f + col_f) * angle) * jnp.sin((row_f - col_f) * angle)
    ends = (index == 0) | (index == order - 1)
    weight = jnp.where(ends, 2.0, 1.0).astype(jnp.float32)
    parity = jnp.where((index[:, None] + index[None, :]) % 2 == 0, 1.0, -1.0).astype(jnp.float32)
    off_diag = index[:, None] != index[None, :]
    safe_diff = jnp.where(off_diag, difference, jnp.float32(1.0))
    entries = jnp.where(
        off_diag, weight[:, None] / weight[None, :] * parity / safe_diff, jnp.float32(0.0)
    )
    entries = entries - jnp.diag(jnp.sum(entries, axis=1))
    mirror = jnp.minimum(index, order - 1 - index).astype(jnp.float32)
    sine = jnp.sin(mirror * (2.0 * angle))
    return -sine[:, None] * entries / (order - 1)


def slot_sum(source, indices, boundary_entry_conductances, total):
    for slot_index in range(indices.shape[1]):
        picked = source[:, indices[:, slot_index], :]
        total = total + boundary_entry_conductances[None, :, slot_index, None] * picked
    return total


def conduct(
    present_solution,
    boundary_group_lookup,
    boundary_entry_conductances,
    exported_boundary_groups,
    spread,
    slab_mask,
    width,
):
    height, plane_vertices = present_solution.shape
    blocks = plane_vertices // width
    face_count = exported_boundary_groups.shape[2]
    blocked = present_solution.reshape(height, blocks, width)
    outgoing = jnp.concatenate(
        [
            blocked[:, exported_boundary_groups[0, 0], :],
            blocked[:, exported_boundary_groups[0, 1], :],
        ],
        axis=1,
    )
    outgoing = outgoing.reshape(height, 2 * face_count * width)
    rim_width = face_count * width
    padded = padded_2(outgoing, (("xs", 1),), rim_width)
    from_left = padded[:, :rim_width].reshape(height, face_count, width)
    from_right = padded[:, padded.shape[1] - rim_width :].reshape(height, face_count, width)
    empty = jnp.zeros((height, 1, width), jnp.float32)
    gathered = jnp.zeros((height, blocks, width), jnp.float32)
    extended = jnp.concatenate([blocked, from_left, from_right, empty], axis=1)
    gathered = slot_sum(extended, boundary_group_lookup, boundary_entry_conductances, gathered)
    coupled = jnp.dot(
        gathered.reshape(-1, spread.shape[0]),
        spread,
        precision=lax.Precision.HIGHEST,
        preferred_element_type=jnp.float32,
    ).reshape(height, plane_vertices)
    return present_solution + slab_mask[None, :] * coupled


def axial(column_field, column_kappa, operator, column_mask):
    slope = jnp.dot(
        operator, column_field, precision=lax.Precision.HIGHEST, preferred_element_type=jnp.float32
    )
    second = jnp.dot(
        operator,
        column_kappa * slope,
        precision=lax.Precision.HIGHEST,
        preferred_element_type=jnp.float32,
    )
    return column_field + axial_step * column_mask[None, :] * second


def to_columns(moved):
    return lax.all_to_all(moved, "hgt", split_axis=1, concat_axis=0, tiled=True)


def to_slabs(result):
    return lax.all_to_all(result, "hgt", split_axis=0, concat_axis=1, tiled=True)


def column_body(
    thermal_field,
    thermal_diffusivity,
    boundary_group_lookup,
    boundary_entry_conductances,
    exported_boundary_groups,
    domain_group_totals,
    pipe_cavity_indicator,
    boundary_vertex_matrix,
):
    layer_sample_number, plane_vertices = thermal_field.shape
    width = boundary_vertex_matrix.shape[0]
    group_size = max(1, 128 // width)
    spread = jnp.kron(jnp.eye(group_size, dtype=jnp.float32), boundary_vertex_matrix)
    block_ids = jnp.arange(plane_vertices) // width
    live_groups = block_ids < domain_group_totals[0]
    slab_mask = jnp.where(live_groups & (pipe_cavity_indicator == 0), 1.0, 0.0).astype(jnp.float32)
    spans = lax.axis_size("hgt")
    column_count = plane_vertices // spans
    column_start = lax.axis_index("hgt") * column_count
    column_mask = lax.dynamic_slice_in_dim(slab_mask, column_start, column_count, 0)
    operator = cheb_matrix(layer_sample_number * spans)
    present_solution = jnp.where(live_groups[None, :], thermal_field, jnp.float32(0.0))
    moved = conduct(
        present_solution,
        boundary_group_lookup,
        boundary_entry_conductances,
        exported_boundary_groups,
        spread,
        slab_mask,
        width,
    )
    column_field, kappa_fixed = (
        lax.all_to_all(moved, "hgt", split_axis=1, concat_axis=0, tiled=True),
        lax.all_to_all(thermal_diffusivity, "hgt", split_axis=1, concat_axis=0, tiled=True),
    )
    result = axial(column_field, kappa_fixed, operator, column_mask)
    present_solution = to_slabs(result)
    moved = conduct(
        present_solution,
        boundary_group_lookup,
        boundary_entry_conductances,
        exported_boundary_groups,
        spread,
        slab_mask,
        width,
    )
    result = axial(to_columns(moved), kappa_fixed, operator, column_mask)
    present_solution = to_slabs(result)
    return present_solution


def body(field, kappa, lookup, conductance, exported, totals, pipe, matrix):
    spans = lax.axis_size("hgt")
    factors = slab_factors(field.shape[0] * spans, spans)
    args = (field, kappa, lookup, conductance, exported, totals, pipe, matrix)
    if factors is None or 2 * matrix.shape[0] != lanes:
        return column_body(*args)
    return slab_body(factors, *args)


def solution(mesh):
    in_specs = (
        P("hgt", ("grp", "xs")),
        P("hgt", ("grp", "xs")),
        P("xs", None),
        P("xs", None),
        P("xs", None, None),
        P("xs"),
        P("xs"),
        P(),
    )
    out_specs = P("hgt", ("grp", "xs"))
    return jax.shard_map(body, mesh=mesh, in_specs=in_specs, out_specs=out_specs, check_vma=False)
```
